32 devices in a mesh: grid: 8 (over y, x, core), ao: 4 (over z).
Axes of the slice: x: 2, y: 2, z: 4, core: 2. Of those that a mesh axis runs over, the one named last changes fastest.
Arguments:
- ao_values: bfloat16 [12288, 12288], P('grid', 'ao'), may hold values from -6 to 6
- coeffs: bfloat16 [12288, 16], P('ao'), may hold values from -0.0546875 to 0.0546875
- screen: int32 [96, 96], P('grid', 'ao'), may hold values 0 or 1
- core_density: float32 [12288], P('grid'), may hold values from 0.3 to 3
- grid_weights: float32 [12288], P('grid'), may hold values from 0.0005 to 0.005
- density_matrix: float32 [12, 16, 16], replicated, as said below
- pair_matrix: bfloat16 [256, 3072], replicated, as said below
Outputs:
- potential: float32 [192, 12288], P(None, 'ao')
The draws below stay inside these ranges and needn't reach their ends.
Inputs may be any that keep to these rules, and one draw needn't show every extreme that they name: `density_matrix`: each state's matrix is symmetric positive definite. `pair_matrix`: each state's 16*16 block is symmetric positive definite.
All inputs are finite; a program needn't handle non-finite values. No bound on the sum of `screen` on one device may be relied on, other than what follows from the above.
Results may differ from the reference program's by a relative error of at most 0.003.
Values may be sent and summed in bfloat16 or wider, within the bound.
A program may use at most 64 MiB of HBM per device.

```python
import math
import jax
import jax.numpy as jnp
from jax import lax

ACT = 16
STATES = 12
NAO = 12288
BLOCK = 128
GRID_PTS = 12288
GRID_BLOCKS = 96
AO_BLOCKS = 96


def draw_density_matrix(key, part):
    key_off, key_diag = jax.random.split(jax.random.fold_in(key, 11))
    off_diag = jax.random.uniform(key_off, (STATES, ACT, ACT), jnp.float32, -0.01, 0.01)
    off_diag = 0.5 * (off_diag + jnp.swapaxes(off_diag, 1, 2))
    base_diag = jax.random.uniform(key_diag, (STATES, ACT), jnp.float32, 0.05, 0.12)
    identity = jnp.eye(ACT, dtype=jnp.float32)
    return off_diag * (1.0 - identity) + identity * (base_diag[:, :, None] + 0.01 * (ACT - 1))


def draw_pair_matrix(key, part):
    key_factor, key_scale = jax.random.split(jax.random.fold_in(key, 23))
    pair_count = ACT * ACT
    factor = jax.random.randint(key_factor, (STATES, pair_count, pair_count), -3, 4).astype(jnp.float32)
    gram = jnp.einsum('sik,sjk->sij', factor, factor, precision=lax.Precision.HIGHEST) / (4.0 * pair_count)
    state_scale = jax.random.uniform(key_scale, (STATES,), jnp.float32, 2.5, 6.0) / pair_count
    identity = jnp.eye(pair_count, dtype=jnp.float32)
    full_matrix = (gram + 0.5 * identity[None, :, :]) * state_scale[:, None, None]
    return jnp.transpose(full_matrix, (1, 0, 2)).reshape(pair_count, STATES * pair_count).astype(jnp.bfloat16)


def touch_ends(drawn, rng, least, high):
    longest = drawn.shape.index(max(drawn.shape))
    spots = []
    for shift in (0, 1):
        where = [jax.random.randint(jax.random.fold_in(rng, axis), (), 0, length) for axis, length in enumerate(drawn.shape)]
        where[longest] = (where[longest] + shift) % drawn.shape[longest]
        spots.append(tuple(where))
    return drawn.at[spots[0]].set(least).at[spots[1]].set(high)


def steps_of(stream_key, shape, cuts, smallest, top_value):
    gain, own = 1.0, jax.random.fold_in(stream_key, 6)
    for dim, parts in cuts:
        heights = jnp.exp(jax.random.uniform(jax.random.fold_in(own, dim), (parts,), jnp.float32, smallest / len(cuts), top_value / len(cuts)))
        gain = gain * jnp.repeat(heights, shape[dim] // parts).reshape([-1 if axis == dim else 1 for axis in range(len(shape))])
    return gain


def normal_values(key, shape, scale, most, cuts=(), held_as=jnp.bfloat16):
    loudness = steps_of(key, shape, cuts, -0.22, 0.18) if cuts else 1.0
    array = jax.random.normal(key, shape, jnp.float32) * scale * loudness
    return jnp.minimum(jnp.maximum(array, -most), most).astype(held_as)


def setup_inputs(seed: int = 0) -> dict:
    streams_of = jax.random.split(jax.random.key(seed), 8)
    ao_values = normal_values(streams_of[0], (GRID_PTS, NAO), 1.0, 6.0, ((0, 8), (1, 4)))
    coeffs = normal_values(streams_of[1], (NAO, ACT), NAO ** -0.5, 0.0546875, ((0, 4),))
    screen = touch_ends((jax.random.randint(streams_of[2], (GRID_BLOCKS, AO_BLOCKS), 0, 3) < 2).astype(jnp.int32), jax.random.fold_in(streams_of[2], 1), 0, 1)
    core_density = jnp.clip(jnp.exp(math.log(3.0) - 2.3025851 * jax.random.uniform(streams_of[3], (GRID_PTS,), jnp.float32) ** steps_of(streams_of[3], (GRID_PTS,), ((0, 8),), -0.2, 0.2)), 0.3, 3.0)
    grid_weights = jnp.clip(jnp.exp(math.log(0.005) - 2.30258502 * jax.random.uniform(streams_of[4], (GRID_PTS,), jnp.float32) ** steps_of(streams_of[4], (GRID_PTS,), ((0, 8),), -0.2, 0.2)), 0.0005, 0.005)
    density_matrix = draw_density_matrix(jax.random.fold_in(streams_of[7], 71), 0)
    pair_matrix = draw_pair_matrix(jax.random.fold_in(streams_of[7], 71), 0)
    return {"ao_values": ao_values, "coeffs": coeffs, "screen": screen, "core_density": core_density, "grid_weights": grid_weights, "density_matrix": density_matrix, "pair_matrix": pair_matrix}


slater_coef = 0.9305257363491
highest = lax.Precision.HIGHEST

def mask_values(ao_values, screen):
    grid_count, basis_count = screen.shape
    height = ao_values.shape[0] // grid_count
    width_cols = ao_values.shape[1] // basis_count
    shaped = ao_values.reshape(grid_count, height, basis_count, width_cols)
    return (shaped * screen.astype(jnp.bfloat16)[:, None, :, None]).reshape(ao_values.shape)

def point_terms(orbitals, core_density, grid_weights, density_matrix, pair_matrix):
    point_count, orbital_count = orbitals.shape
    state_count = density_matrix.shape[0]
    pair_count = orbital_count * orbital_count
    pair_values = (orbitals[:, :, None] * orbitals[:, None, :]).reshape(point_count, pair_count).astype(jnp.bfloat16)
    pair_image = jnp.dot(pair_values, pair_matrix, preferred_element_type=jnp.float32).reshape(point_count, state_count, pair_count)
    on_top = jnp.einsum('bk,bsk->bs', pair_values.astype(jnp.float32), pair_image, precision=highest)
    density_grad = jnp.einsum('spq,bq->bsp', density_matrix, orbitals, precision=highest)
    density = core_density[:, None] + jnp.einsum('bp,bsp->bs', orbitals, density_grad, precision=highest)
    pair_ratio = 4.0 * on_top / (density * density)
    unclamped = jnp.where(pair_ratio < 1.0, 1.0, 0.0).astype(jnp.float32)
    polarize = jnp.sqrt(jnp.clip(1.0 - pair_ratio, 0.0, 1.0))
    upper_root = (1.0 + polarize) ** (1.0 / 3.0)
    lower_root = (1.0 - polarize) ** (1.0 / 3.0)
    enhance = upper_root ** 4 + lower_root ** 4
    slope = 4.0 / 3.0 / (upper_root * upper_root + upper_root * lower_root + lower_root * lower_root)
    half_cube = (0.5 * density) ** (1.0 / 3.0)
    quartic = half_cube ** 4
    pot_pair = 4.0 * slater_coef * quartic * slope * unclamped / (density * density)
    pot_density = -(2.0 / 3.0) * slater_coef * half_cube * enhance - 8.0 * slater_coef * quartic * slope * unclamped * on_top / (density * density * density)
    pair_square = pair_image.reshape(point_count, state_count, orbital_count, orbital_count)
    pair_sym = pair_square + jnp.swapaxes(pair_square, 2, 3)
    pair_grad = jnp.einsum('bspq,bq->bsp', pair_sym, orbitals, precision=highest)
    orbital_grad = grid_weights[:, None, None] * (pot_density[:, :, None] * density_grad + pot_pair[:, :, None] * pair_grad)
    return orbital_grad.reshape(point_count, state_count * orbital_count).astype(jnp.bfloat16)

def reference(ao_values, coeffs, screen, core_density, grid_weights, density_matrix, pair_matrix):
    row_block = 512 if GRID_PTS % 512 == 0 else BLOCK
    block_count = GRID_PTS // row_block

    def advance(running, pieces):
        values, marks, core_piece, weight_piece = pieces
        masked = mask_values(values, marks)
        orbitals = jnp.dot(masked, coeffs, preferred_element_type=jnp.float32)
        gradient = point_terms(orbitals, core_piece, weight_piece, density_matrix, pair_matrix)
        update = lax.dot_general(gradient, masked, (((0,), (0,)), ((), ())), preferred_element_type=jnp.float32)
        return (running + update, None)
    initial = jnp.zeros((STATES * ACT, NAO), jnp.float32)
    pieces = (ao_values.reshape(block_count, row_block, NAO), screen.reshape(block_count, row_block // BLOCK, AO_BLOCKS), core_density.reshape(block_count, row_block), grid_weights.reshape(block_count, row_block))
    potential, unused = lax.scan(advance, initial, pieces)
    return potential
```

```python
import functools

import jax
import jax.numpy as jnp
from jax import lax
from jax.experimental import pallas as pl
from jax.experimental.pallas import tpu as pltpu
from jax.sharding import PartitionSpec as P

slater_coef = 0.9305257363491
highest = lax.Precision.HIGHEST


def mask_values(ao_values, screen):
    grid_count, basis_count = screen.shape
    height = ao_values.shape[0] // grid_count
    width_cols = ao_values.shape[1] // basis_count
    shaped = ao_values.reshape(grid_count, height, basis_count, width_cols)
    return (shaped * screen.astype(jnp.bfloat16)[:, None, :, None]).reshape(ao_values.shape)


def point_terms(orbitals, core_density, grid_weights, density_matrix, pair_matrix):
    point_count, orbital_count = orbitals.shape
    state_count = density_matrix.shape[0]
    pair_count = orbital_count * orbital_count
    pair_values = (
        (orbitals[:, :, None] * orbitals[:, None, :])
        .reshape(point_count, pair_count)
        .astype(jnp.bfloat16)
    )
    pair_image = jnp.dot(pair_values, pair_matrix, preferred_element_type=jnp.float32).reshape(
        point_count, state_count, pair_count
    )
    on_top = jnp.einsum(
        "bk,bsk->bs", pair_values.astype(jnp.float32), pair_image, precision=highest
    )
    density_grad = jnp.einsum("spq,bq->bsp", density_matrix, orbitals, precision=highest)
    density = core_density[:, None] + jnp.einsum(
        "bp,bsp->bs", orbitals, density_grad, precision=highest
    )
    pair_ratio = 4.0 * on_top / (density * density)
    unclamped = jnp.where(pair_ratio < 1.0, 1.0, 0.0).astype(jnp.float32)
    polarize = jnp.sqrt(jnp.clip(1.0 - pair_ratio, 0.0, 1.0))
    upper_root = (1.0 + polarize) ** (1.0 / 3.0)
    lower_root = (1.0 - polarize) ** (1.0 / 3.0)
    enhance = upper_root**4 + lower_root**4
    slope = (
        4.0 / 3.0 / (upper_root * upper_root + upper_root * lower_root + lower_root * lower_root)
    )
    half_cube = (0.5 * density) ** (1.0 / 3.0)
    quartic = half_cube**4
    pot_pair = 4.0 * slater_coef * quartic * slope * unclamped / (density * density)
    pot_density = -(
        2.0 / 3.0
    ) * slater_coef * half_cube * enhance - 8.0 * slater_coef * quartic * slope * unclamped * on_top / (
        density * density * density
    )
    pair_square = pair_image.reshape(point_count, state_count, orbital_count, orbital_count)
    pair_sym = pair_square + jnp.swapaxes(pair_square, 2, 3)
    pair_grad = jnp.einsum("bspq,bq->bsp", pair_sym, orbitals, precision=highest)
    orbital_grad = grid_weights[:, None, None] * (
        pot_density[:, :, None] * density_grad + pot_pair[:, :, None] * pair_grad
    )
    return orbital_grad.reshape(point_count, state_count * orbital_count).astype(jnp.bfloat16)


def blocked_terms(orbitals, core_density, grid_weights, density_matrix, pair_matrix):
    point_count = orbitals.shape[0]
    row_block = 512
    block_count = point_count // row_block
    pieces = (
        orbitals.reshape(block_count, row_block, orbitals.shape[1]),
        core_density.reshape(block_count, row_block),
        grid_weights.reshape(block_count, row_block),
    )
    stacked = lax.map(
        lambda items: point_terms(items[0], items[1], items[2], density_matrix, pair_matrix), pieces
    )
    return stacked.reshape(point_count, stacked.shape[2])


def contract_rows(gradient, values):
    return lax.dot_general(
        gradient, values, (((0,), (0,)), ((), ())), preferred_element_type=jnp.float32
    )


def local(ao_values, coeffs, screen, core_density, grid_weights, density_matrix, pair_matrix):
    masked = mask_values(ao_values, screen)
    orbitals = lax.psum(jnp.dot(masked, coeffs, preferred_element_type=jnp.float32), "ao")
    gradient = blocked_terms(orbitals, core_density, grid_weights, density_matrix, pair_matrix)
    partial_pot = contract_rows(gradient, masked)
    return lax.psum(partial_pot, "grid")


bf16, f32 = jnp.bfloat16, jnp.float32
MESH = pl.DeviceIdType.MESH
AO, GRID = 4, 8
CUT = 2


def parts3(v):
    a = v.astype(bf16)
    r = v - a.astype(f32)
    b = r.astype(bf16)
    return a, b, (r - b.astype(f32)).astype(bf16)


def kernel(ao_hbm, coeffs, screen, core_den, weights, dens, pair_hbm, out_hbm,
           ao, pair, mat, pv, dmat, dg, tgrad, on_top, den, grad, rs_send, rs_recv, orb,
           s1_send, s1_recv, s2_send, s2_recv, s3_send, s3_recv, keep, gath,
           ld_sem, rs_ss, rs_rs, ag_ss, ag_rs, s1_ss, s1_rs, s2_ss, s2_rs, s3_ss, s3_rs,
           g3_ss, g3_rs, g2_ss, g2_rs, g1_ss, g1_rs, pair_sem, out_sem):
    points, cols = ao.shape
    states = mat.shape[0]
    act = orb.shape[1]
    pairs = act * act
    rows = states * act
    seg = points // AO
    half, quarter, eighth = cols // 2, cols // 4, cols // 8
    za = lax.axis_index("ao")
    g = lax.axis_index("grid")
    core, x, y = lax.rem(g, 2), lax.rem(g // 2, 2), g // 4
    b2 = x * (1 - core) + y * core
    b3 = y * (1 - core) + x * core
    p1 = g + 1 - 2 * core
    p2 = g + (1 - core) * (2 - 4 * x) + core * (4 - 8 * y)
    p3 = g + core * (2 - 4 * x) + (1 - core) * (4 - 8 * y)

    loads = []
    for k in range(AO):
        r = lax.rem(za + 1 + k, AO)
        start = pl.multiple_of(r * seg, seg)
        cp = pltpu.make_async_copy(ao_hbm.at[pl.ds(start, seg)], ao.at[pl.ds(start, seg)], ld_sem.at[k])
        cp.start()
        loads.append((cp, r, start))

    pair_load = pltpu.make_async_copy(pair_hbm, pair, pair_sem)
    pair_load.start()
    barrier = pltpu.get_barrier_semaphore()
    for k in range(1, AO):
        pl.semaphore_signal(barrier, inc=1, device_id={"ao": lax.rem(za + k, AO)}, device_id_type=MESH)
    for p in (p1, p2, p3):
        pl.semaphore_signal(barrier, inc=1, device_id={"grid": p}, device_id_type=MESH)

    per = seg // 128
    cf = coeffs[...]
    sends = []
    for k in range(AO):
        cp, r, start = loads[k]
        cp.wait()

        def mask(i, c):
            at = pl.multiple_of(start + i * 128, 128)
            for j in range(cols // 128):
                m = jnp.full((128, 128), screen[r * per + i, j].astype(f32)).astype(bf16)
                ao[pl.ds(at, 128), j * 128:(j + 1) * 128] = ao[pl.ds(at, 128), j * 128:(j + 1) * 128] * m
            return c

        lax.fori_loop(0, per, mask, 0)
        rs_send[k] = lax.dot_general(
            cf, ao[pl.ds(start, seg), :], (((1,), (1,)), ((), ())), preferred_element_type=f32)
        if k == 0:
            pl.semaphore_wait(barrier, AO - 1 + 3)
        if k < AO - 1:
            rc = pltpu.make_async_remote_copy(
                src_ref=rs_send.at[k], dst_ref=rs_recv.at[k], send_sem=rs_ss.at[k], recv_sem=rs_rs.at[k],
                device_id={"ao": r}, device_id_type=MESH)
            rc.start()
            sends.append(rc)
    ri = lax.broadcasted_iota(jnp.int32, (pairs, pairs), 0)
    ci = lax.broadcasted_iota(jnp.int32, (pairs, pairs), 1)
    perm = jnp.where(ci == lax.rem(ri, act) * act + ri // act, 1.0, 0.0).astype(bf16)

    def swap(s, c):
        blk = pair[:, pl.ds(pl.multiple_of(s * pairs, pairs), pairs)]
        mat[s, :, 0:pairs] = blk
        mat[s, :, pairs:] = jnp.dot(perm, blk, preferred_element_type=f32).astype(bf16)
        return c

    pair_load.wait()
    lax.fori_loop(0, states, swap, 0)
    d1, d2, d3 = parts3(dens[...])
    dmat[...] = jnp.concatenate([v.astype(f32) for v in (d1, d1, d2, d2, d1, d3)], axis=1).astype(bf16)
    total = rs_send[AO - 1]
    for k in range(AO - 1):
        sends[k].wait_recv()
        total = total + rs_recv[k]
    orb[0] = total

    def gather_copy(k):
        return pltpu.make_async_remote_copy(
            src_ref=orb.at[0], dst_ref=orb.at[k], send_sem=ag_ss.at[k], recv_sem=ag_rs.at[k],
            device_id={"ao": lax.rem(za + k, AO)}, device_id_type=MESH)

    gathers = [gather_copy(k) for k in range(1, AO)]
    for rc in gathers:
        rc.start()

    def terms(k, c):
        o = orb[k]
        start = pl.multiple_of(lax.rem(za - k + AO, AO) * seg, seg)
        for p in range(act):
            v = (o[p:p + 1, :] * o).astype(bf16)
            pv[p * act:(p + 1) * act, :] = v
            pv[pairs + p * act:pairs + (p + 1) * act, :] = v
        o1, o2, o3 = parts3(o)
        dg[...] = jnp.dot(dmat[...], jnp.concatenate([o1, o2, o1, o2, o3, o1], axis=0), preferred_element_type=f32)

        image = jnp.dot(mat[...].reshape(states * pairs, 2 * pairs), pv[...], preferred_element_type=f32)
        for s in range(states):
            t = jnp.zeros((act, seg), f32)
            ot = jnp.zeros((act, seg), f32)
            for q in range(act):
                piece = image[s * pairs + q * act:s * pairs + (q + 1) * act, :]
                t = t + piece * o[q:q + 1, :]
                ot = ot + piece * pv[q * act:(q + 1) * act, :].astype(f32)
            at = s * act
            tgrad[at:at + act, :] = t
            on_top[s:s + 1, :] = 0.5 * jnp.sum(ot, axis=0, keepdims=True)
            den[s:s + 1, :] = jnp.sum(o * dg[at:at + act, :], axis=0, keepdims=True)
        third = 1.0 / 3.0
        top = on_top[...]
        density = core_den[pl.ds(start, seg)].reshape(1, seg) + den[...]
        ratio = 4.0 * top / (density * density)
        unclamped = jnp.where(ratio < 1.0, 1.0, 0.0)
        polarize = jnp.sqrt(jnp.minimum(jnp.maximum(1.0 - ratio, 0.0), 1.0))
        upper = jnp.exp(jnp.log(1.0 + polarize) * third)
        lower = jnp.exp(jnp.log(1.0 - polarize) * third)
        u2, l2 = upper * upper, lower * lower
        enhance = u2 * u2 + l2 * l2
        slope = 4.0 / 3.0 / (u2 + upper * lower + l2)
        hc = jnp.exp(jnp.log(0.5 * density) * third)
        h2 = hc * hc
        base = 4.0 * slater_coef * (h2 * h2) * slope * unclamped / (density * density)
        pot_den = -(2.0 / 3.0) * slater_coef * hc * enhance - 2.0 * base * top / density
        w = weights[pl.ds(start, seg)].reshape(1, seg)
        on_top[...] = base * w
        den[...] = pot_den * w
        for s in range(states):
            at = s * act
            grad[at:at + act, pl.ds(start, seg)] = (
                den[s:s + 1, :] * dg[at:at + act, :] + on_top[s:s + 1, :] * tgrad[at:at + act, :]
            ).astype(bf16)
        return c

    for k in range(AO):
        if k:
            gathers[k - 1].wait_recv()
        terms(k, 0)

    def pot(off, width):
        return jnp.dot(grad[...], ao[:, pl.ds(pl.multiple_of(off, eighth), width)], preferred_element_type=f32)

    def send(src, dst, ss, rs, p):
        rc = pltpu.make_async_remote_copy(
            src_ref=src, dst_ref=dst, send_sem=ss, recv_sem=rs, device_id={"grid": p}, device_id_type=MESH)
        rc.start()
        return rc

    own, other = core * half, (1 - core) * half
    c1 = []
    for i, b in ((0, 1 - b3), (1, b3)):
        s1_send[i] = pot(other + b * quarter, quarter)
        c1.append(send(s1_send.at[i], s1_recv.at[i], s1_ss.at[i], s1_rs.at[i], p1))
    for i, b in ((0, 1 - b3), (1, b3)):
        keep[i] = pot(own + (1 - b2) * quarter + b * eighth, eighth)
    piece = rows // CUT
    at_row = [slice(c * piece, (c + 1) * piece) for c in range(CUT)]
    c2, c3 = [[], []], []
    c1[0].wait_recv()
    for i, b in ((0, 1 - b3), (1, b3)):
        for c, r in enumerate(at_row):
            s2_send[i, r] = (
                keep[i, r] + s1_recv[0, r, pl.ds(pl.multiple_of(b * eighth, eighth), eighth)]).astype(bf16)
            c2[i].append(send(s2_send.at[i, r], s2_recv.at[i, r], s2_ss.at[i, c], s2_rs.at[i, c], p2))
    for i, b in ((0, 1 - b3), (1, b3)):
        keep[i] = pot(own + b2 * quarter + b * eighth, eighth)
    c1[1].wait_recv()
    for i, b in ((0, 1 - b3), (1, b3)):
        keep[i] += s1_recv[1, :, pl.ds(pl.multiple_of(b * eighth, eighth), eighth)]
    for c, r in enumerate(at_row):
        c2[0][c].wait_recv()
        s3_send[r] = (keep[0, r] + s2_recv[0, r].astype(f32)).astype(bf16)
        c3.append(send(s3_send.at[r], s3_recv.at[r], s3_ss.at[c], s3_rs.at[c], p3))
    e_own = core * 4 + b2 * 2 + b3
    e_3 = core * 4 + b2 * 2 + 1 - b3
    e_2 = core * 4 + (1 - b2) * 2 + b3
    e_23 = core * 4 + (1 - b2) * 2 + 1 - b3
    outs = []

    def put(e, c):
        r = at_row[c]
        cp = pltpu.make_async_copy(
            gath.at[e, r], out_hbm.at[r, pl.ds(pl.multiple_of(e * eighth, eighth), eighth)], out_sem.at[len(outs)])
        cp.start()
        outs.append(cp)

    def share(e, c, ss, rs, p):
        return send(gath.at[e, at_row[c]], gath.at[e, at_row[c]], ss, rs, p)

    f3, f2a, f2b, f1 = [], [], [], [[], [], [], []]
    for c, r in enumerate(at_row):
        c2[1][c].wait_recv()
        c3[c].wait_recv()
        gath[e_own, r] = (keep[1, r] + s2_recv[1, r].astype(f32) + s3_recv[r].astype(f32)).astype(bf16)
        f3.append(share(e_own, c, g3_ss.at[c], g3_rs.at[c], p3))
        f2a.append(share(e_own, c, g2_ss.at[0, c], g2_rs.at[0, c], p2))
        f1[0].append(share(e_own, c, g1_ss.at[0, c], g1_rs.at[0, c], p1))
        put(e_own, c)
    for c in range(CUT):
        f3[c].wait_recv()
        f2b.append(share(e_3, c, g2_ss.at[1, c], g2_rs.at[1, c], p2))
        f1[1].append(share(e_3, c, g1_ss.at[1, c], g1_rs.at[1, c], p1))
        put(e_3, c)
    for c in range(CUT):
        f2a[c].wait_recv()
        f1[2].append(share(e_2, c, g1_ss.at[2, c], g1_rs.at[2, c], p1))
        put(e_2, c)
    for c in range(CUT):
        f2b[c].wait_recv()
        f1[3].append(share(e_23, c, g1_ss.at[3, c], g1_rs.at[3, c], p1))
        put(e_23, c)
    base_e = (1 - core) * 4
    for i, e in enumerate((b3 * 2 + b2, b3 * 2 + 1 - b2, (1 - b3) * 2 + b2, (1 - b3) * 2 + 1 - b2)):
        for c in range(CUT):
            f1[i][c].wait_recv()
            put(base_e + e, c)
    for rc in sends + gathers + c1 + c2[0] + c2[1] + c3 + f3 + f2a + f2b + f1[0] + f1[1] + f1[2] + f1[3]:
        rc.wait_send()
    for cp in outs:
        cp.wait()


def local_kernel(ao_values, coeffs, screen, core_density, grid_weights, density_matrix, pair_matrix):
    points, cols = ao_values.shape
    states, act = density_matrix.shape[0], density_matrix.shape[1]
    pairs, rows = act * act, states * act
    seg, quarter, eighth = points // AO, cols // 4, cols // 8
    vm, hbm = pl.BlockSpec(memory_space=pltpu.VMEM), pl.BlockSpec(memory_space=pl.ANY)
    dma, V = pltpu.SemaphoreType.DMA, pltpu.VMEM
    return pl.pallas_call(
        kernel,
        out_shape=jax.ShapeDtypeStruct((rows, cols), bf16),
        in_specs=[hbm, vm, pl.BlockSpec(memory_space=pltpu.SMEM), vm, vm, vm, hbm],
        out_specs=vm,
        scratch_shapes=[
            V((points, cols), bf16), V(pair_matrix.shape, bf16), V((states, pairs, 2 * pairs), bf16), V((2 * pairs, seg), bf16),
            V((rows, 6 * act), bf16), V((rows, seg), f32), V((rows, seg), f32),
            V((states, seg), f32), V((states, seg), f32), V((rows, points), bf16),
            V((AO, act, seg), f32), V((AO, act, seg), f32), V((AO, act, seg), f32),
            V((2, rows, quarter), f32), V((2, rows, quarter), f32),
            V((2, rows, eighth), bf16), V((2, rows, eighth), bf16),
            V((rows, eighth), bf16), V((rows, eighth), bf16),
            V((2, rows, eighth), f32), V((8, rows, eighth), bf16),
            dma((AO,)), dma((AO,)), dma((AO,)), dma((AO,)), dma((AO,)),
            dma((2,)), dma((2,)), dma((2, CUT)), dma((2, CUT)), dma((CUT,)), dma((CUT,)),
            dma((CUT,)), dma((CUT,)), dma((2, CUT)), dma((2, CUT)), dma((4, CUT)), dma((4, CUT)),
            dma, dma((8 * CUT,)),
        ],
        compiler_params=pltpu.CompilerParams(
            collective_id=0, has_side_effects=True, vmem_limit_bytes=40 * 2**20),
    )(*[pltpu.with_memory_space_constraint(v, pltpu.HBM) for v in (
        ao_values, coeffs.T, screen, core_density, grid_weights,
        density_matrix.reshape(rows, act), pair_matrix)]).astype(f32)


def solution(mesh):
    fits = mesh.shape["grid"] == GRID and mesh.shape["ao"] == AO
    in_specs = (P("grid", "ao"), P("ao", None), P("grid", "ao"), P("grid"), P("grid"), P(), P())
    out_specs = P(None, "ao")
    return jax.shard_map(local_kernel if fits else local, mesh=mesh, in_specs=in_specs, out_specs=out_specs, check_vma=False)
```

```python
import functools

import jax
import jax.numpy as jnp
from jax import lax
from jax.experimental import pallas as pl
from jax.experimental.pallas import tpu as pltpu
from jax.sharding import PartitionSpec as P

slater_coef = 0.9305257363491
highest = lax.Precision.HIGHEST


def mask_values(ao_values, screen):
    grid_count, basis_count = screen.shape
    height = ao_values.shape[0] // grid_count
    width_cols = ao_values.shape[1] // basis_count
    shaped = ao_values.reshape(grid_count, height, basis_count, width_cols)
    return (shaped * screen.astype(jnp.bfloat16)[:, None, :, None]).reshape(ao_values.shape)


def point_terms(orbitals, core_density, grid_weights, density_matrix, pair_matrix):
    point_count, orbital_count = orbitals.shape
    state_count = density_matrix.shape[0]
    pair_count = orbital_count * orbital_count
    pair_values = (
        (orbitals[:, :, None] * orbitals[:, None, :])
        .reshape(point_count, pair_count)
        .astype(jnp.bfloat16)
    )
    pair_image = jnp.dot(pair_values, pair_matrix, preferred_element_type=jnp.float32).reshape(
        point_count, state_count, pair_count
    )
    on_top = jnp.einsum(
        "bk,bsk->bs", pair_values.astype(jnp.float32), pair_image, precision=highest
    )
    density_grad = jnp.einsum("spq,bq->bsp", density_matrix, orbitals, precision=highest)
    density = core_density[:, None] + jnp.einsum(
        "bp,bsp->bs", orbitals, density_grad, precision=highest
    )
    pair_ratio = 4.0 * on_top / (density * density)
    unclamped = jnp.where(pair_ratio < 1.0, 1.0, 0.0).astype(jnp.float32)
    polarize = jnp.sqrt(jnp.clip(1.0 - pair_ratio, 0.0, 1.0))
    upper_root = (1.0 + polarize) ** (1.0 / 3.0)
    lower_root = (1.0 - polarize) ** (1.0 / 3.0)
    enhance = upper_root**4 + lower_root**4
    slope = (
        4.0 / 3.0 / (upper_root * upper_root + upper_root * lower_root + lower_root * lower_root)
    )
    half_cube = (0.5 * density) ** (1.0 / 3.0)
    quartic = half_cube**4
    pot_pair = 4.0 * slater_coef * quartic * slope * unclamped / (density * density)
    pot_density = -(
        2.0 / 3.0
    ) * slater_coef * half_cube * enhance - 8.0 * slater_coef * quartic * slope * unclamped * on_top / (
        density * density * density
    )
    pair_square = pair_image.reshape(point_count, state_count, orbital_count, orbital_count)
    pair_sym = pair_square + jnp.swapaxes(pair_square, 2, 3)
    pair_grad = jnp.einsum("bspq,bq->bsp", pair_sym, orbitals, precision=highest)
    orbital_grad = grid_weights[:, None, None] * (
        pot_density[:, :, None] * density_grad + pot_pair[:, :, None] * pair_grad
    )
    return orbital_grad.reshape(point_count, state_count * orbital_count).astype(jnp.bfloat16)


def blocked_terms(orbitals, core_density, grid_weights, density_matrix, pair_matrix):
    point_count = orbitals.shape[0]
    row_block = 512
    block_count = point_count // row_block
    pieces = (
        orbitals.reshape(block_count, row_block, orbitals.shape[1]),
        core_density.reshape(block_count, row_block),
        grid_weights.reshape(block_count, row_block),
    )
    stacked = lax.map(
        lambda items: point_terms(items[0], items[1], items[2], density_matrix, pair_matrix), pieces
    )
    return stacked.reshape(point_count, stacked.shape[2])


def contract_rows(gradient, values):
    return lax.dot_general(
        gradient, values, (((0,), (0,)), ((), ())), preferred_element_type=jnp.float32
    )


def local(ao_values, coeffs, screen, core_density, grid_weights, density_matrix, pair_matrix):
    masked = mask_values(ao_values, screen)
    orbitals = lax.psum(jnp.dot(masked, coeffs, preferred_element_type=jnp.float32), "ao")
    gradient = blocked_terms(orbitals, core_density, grid_weights, density_matrix, pair_matrix)
    partial_pot = contract_rows(gradient, masked)
    return lax.psum(partial_pot, "grid")


bf16, f32 = jnp.bfloat16, jnp.float32
MESH = pl.DeviceIdType.MESH
AO, GRID = 4, 8
BLK = 128
EARLY, CUT = 1, 4


def parts3(v):
    a = v.astype(bf16)
    r = v - a.astype(f32)
    b = r.astype(bf16)
    return a, b, (r - b.astype(f32)).astype(bf16)


def pair_row(index, act):
    first = index % act
    second = (first + index // act) % act
    return first * act + second, second * act + first


def ones_where(cond):
    return jnp.where(cond, 1.0, 0.0)


def kernel(ao_hbm, cf_hbm, screen_hbm, core_hbm, weights_hbm, dens_hbm, pair_hbm, out,
           ao, coeffs, screen, core_den, weights, dens, pair, mask, mcf, mat, pv, pvf, orot, dmat, dg,
           tgrad, top, den, grad, rs_send, rs_recv, orb, whole, s1_send, s1_recv, s2_send, s2_recv, s3_send, s3_recv,
           keep, gath, ld_sem, rs_ss, rs_rs, ag_ss, ag_rs, x_ss, x_rs):
    points, cols = ao.shape
    act = orb.shape[2]
    shifts = act // 2 + 1
    packed = shifts * act
    rows = dens.shape[0]
    states = rows // act
    pairs = act * act
    wide = AO * BLK
    groups = points // wide
    half, quarter, eighth = cols // 2, cols // 4, cols // 8
    za = lax.axis_index("ao")
    g = lax.axis_index("grid")
    core, x, y = lax.rem(g, 2), lax.rem(g // 2, 2), g // 4
    h = lax.rem(core + x + y, 2)
    b2 = x * (1 - h) + y * h
    b3 = y * (1 - h) + x * h
    p1 = g + 1 - 2 * core
    p2 = p1 + (1 - h) * (2 - 4 * x) + h * (4 - 8 * y)
    p3 = p1 + h * (2 - 4 * x) + (1 - h) * (4 - 8 * y)

    barrier = pltpu.get_barrier_semaphore()
    for k in range(1, AO):
        pl.semaphore_signal(barrier, inc=1, device_id={"ao": lax.rem(za + k, AO)}, device_id_type=MESH)
    for p in (p1, p2, p3):
        pl.semaphore_signal(barrier, inc=1, device_id={"grid": p}, device_id_type=MESH)

    def load(src, dst, i):
        cp = pltpu.make_async_copy(src, dst, ld_sem.at[i])
        cp.start()
        return cp

    step = 2 * BLK
    small = [load(s, d, i) for i, (s, d) in enumerate(((cf_hbm, coeffs), (screen_hbm, screen)))]
    loads = [load(ao_hbm.at[pl.ds(i * step, step)], ao.at[pl.ds(i * step, step)], 2 + i) for i in range(points // step)]
    late = [load(s, d, 2 + len(loads) + i) for i, (s, d) in enumerate(
        ((pair_hbm, pair), (dens_hbm, dens), (core_hbm, core_den), (weights_hbm, weights)))]

    for cp in small:
        cp.wait()
    cf = coeffs[...]
    marks = screen[...].astype(f32)
    for j in range(cols // BLK):
        v = jnp.broadcast_to(marks[:, j:j + 1], (points // BLK, BLK))
        for i in range(points // BLK):
            mask[i, :, j * BLK:(j + 1) * BLK] = jnp.broadcast_to(v[i:i + 1, :], (act, BLK)).astype(bf16)
    for i in range(points // BLK):
        mcf[i * act:(i + 1) * act, :] = cf * mask[i]

    def z_copy(src, dst, ss, rs, t, k):
        return pltpu.make_async_remote_copy(
            src_ref=src, dst_ref=dst, send_sem=ss.at[t, k - 1], recv_sem=rs.at[t, k - 1],
            device_id={"ao": lax.rem(za + k, AO)}, device_id_type=MESH)

    def scatter_copy(t, k):
        return z_copy(rs_send.at[t, lax.rem(za + k, AO)], rs_recv.at[t, k - 1], rs_ss, rs_rs, t, k)

    def gather_copy(t, k):
        return z_copy(orb.at[t, za], orb.at[t, za], ag_ss, ag_rs, t, k)

    def whole_copy(t, k):
        return z_copy(whole.at[t - EARLY, za], whole.at[t - EARLY, za], rs_ss, rs_rs, t, k)

    for t in range(groups):
        for u in range(2):
            i = 2 * t + u
            loads[i].wait()
            r = lax.dot_general(mcf[2 * i * act:2 * (i + 1) * act, :], ao[i * step:(i + 1) * step, :],
                                (((1,), (1,)), ((), ())), preferred_element_type=f32)
            if t < EARLY:
                rs_send[t, 2 * u] = r[0:act, 0:BLK]
                rs_send[t, 2 * u + 1] = r[act:, BLK:]
            else:
                whole[t - EARLY, za, :, u * step:u * step + BLK] = r[0:act, 0:BLK]
                whole[t - EARLY, za, :, u * step + BLK:(u + 1) * step] = r[act:, BLK:]
        if t == 0:
            pl.semaphore_wait(barrier, AO - 1 + 3)
        for k in range(1, AO):
            (scatter_copy(t, k) if t < EARLY else whole_copy(t, k)).start()

    for cp in late:
        cp.wait()
    d1, d2, d3 = parts3(dens[...])
    dmat[...] = jnp.concatenate([v.astype(f32) for v in (d1, d1, d2, d2, d1, d3)], axis=1).astype(bf16)
    fp, fq = pair_row(lax.broadcasted_iota(jnp.int32, (packed, pairs), 0), act)
    ci = lax.broadcasted_iota(jnp.int32, (packed, pairs), 1)
    fold_rows = (ones_where(ci == fp) + ones_where(ci == fq)).astype(bf16)
    few = 3
    for b in range(states // few):
        folded = jnp.dot(fold_rows, pair[:, b * few * pairs:(b + 1) * few * pairs], preferred_element_type=f32)
        hi = folded.astype(bf16)
        lo = (folded - hi.astype(f32)).astype(bf16)
        for i in range(few):
            mat[b * few + i, :, 0:pairs] = hi[:, i * pairs:(i + 1) * pairs]
            mat[b * few + i, :, pairs:] = lo[:, i * pairs:(i + 1) * pairs]

    def screen_rows(i, c):
        at = pl.multiple_of(i * BLK, BLK)
        for j in range(cols // BLK):
            m = jnp.concatenate([mask[i, :, j * BLK:(j + 1) * BLK]] * (BLK // mask.shape[1]), axis=0)
            ao[pl.ds(at, BLK), j * BLK:(j + 1) * BLK] = ao[pl.ds(at, BLK), j * BLK:(j + 1) * BLK] * m
        return c

    lax.fori_loop(0, 2, screen_rows, 0)
    for t in range(EARLY):
        total = rs_send[t, za]
        for k in range(1, AO):
            scatter_copy(t, k).wait_recv()
            total = total + rs_recv[t, k - 1]
        orb[t, za] = total
        for k in range(1, AO):
            gather_copy(t, k).start()
    lax.fori_loop(2, points // BLK, screen_rows, 0)

    def prepare(t):
        o = orot[t, 0:act, :]
        for d in range(shifts):
            od = o if d == 0 else jnp.concatenate([o[d:], o[:d]], axis=0)
            if d:
                orot[t, d * act:(d + 1) * act, :] = od
            v = (o * od).astype(bf16)
            edge = d == 0 or d == shifts - 1
            pvf[t, d * act:(d + 1) * act, :] = v.astype(f32) * (0.5 if edge else 1.0)
        for p in range(act):
            v = (o[p:p + 1, :] * o).astype(bf16)
            pv[t, p * act:(p + 1) * act, :] = v
            pv[t, pairs + p * act:pairs + (p + 1) * act, :] = v
        o1, o2, o3 = parts3(o)
        dg[t] = jnp.dot(dmat[...], jnp.concatenate([o1, o2, o1, o2, o3, o1], axis=0), preferred_element_type=f32)

    def terms(t):
        o = orot[t, 0:act, :]
        image = jnp.dot(mat[...].reshape(states * packed, mat.shape[2]), pv[t], preferred_element_type=f32)
        for s in range(states):
            z = [image[s * packed + d * act:s * packed + (d + 1) * act, :] for d in range(shifts)]
            ot = z[0] * pvf[t, 0:act, :]
            tg = z[0] * o
            for d in range(1, shifts):
                ot = ot + z[d] * pvf[t, d * act:(d + 1) * act, :]
                tg = tg + z[d] * orot[t, d * act:(d + 1) * act, :]
            back = z[shifts - 2] * o
            for d in range(shifts - 3, -1, -1):
                back = jnp.concatenate([back[act - 1:], back[:act - 1]], axis=0)
                if d:
                    back = back + z[d] * o
            at = s * act
            tgrad[at:at + act, :] = tg + back
            top[s:s + 1, :] = jnp.sum(ot, axis=0, keepdims=True)
            den[s:s + 1, :] = jnp.sum(o * dg[t, at:at + act, :], axis=0, keepdims=True)
        start = pl.multiple_of(t * wide, wide)
        third = 1.0 / 3.0
        on_top = top[...]
        density = core_den[pl.ds(start, wide)].reshape(1, wide) + den[...]
        ratio = 4.0 * on_top / (density * density)
        unclamped = jnp.where(ratio < 1.0, 1.0, 0.0)
        polarize = jnp.sqrt(jnp.minimum(jnp.maximum(1.0 - ratio, 0.0), 1.0))
        upper = jnp.exp(jnp.log(1.0 + polarize) * third)
        lower = jnp.exp(jnp.log(1.0 - polarize) * third)
        u2, l2 = upper * upper, lower * lower
        enhance = u2 * u2 + l2 * l2
        slope = 4.0 / 3.0 / (u2 + upper * lower + l2)
        hc = jnp.exp(jnp.log(0.5 * density) * third)
        h2 = hc * hc
        base = 4.0 * slater_coef * (h2 * h2) * slope * unclamped / (density * density)
        pot_den = -(2.0 / 3.0) * slater_coef * hc * enhance - 2.0 * base * on_top / density
        w = weights[pl.ds(start, wide)].reshape(1, wide)
        top[...] = base * w
        den[...] = pot_den * w
        for s in range(states):
            at = s * act
            grad[at:at + act, pl.ds(start, wide)] = (
                den[s:s + 1, :] * dg[t, at:at + act, :] + top[s:s + 1, :] * tgrad[at:at + act, :]
            ).astype(bf16)

    cut = rows // CUT
    cuts = [slice(k * cut, (k + 1) * cut) for k in range(CUT)]
    sent = []

    def send(src, dst, p):
        i = len(sent)
        rc = pltpu.make_async_remote_copy(
            src_ref=src, dst_ref=dst, send_sem=x_ss.at[i], recv_sem=x_rs.at[i], device_id={"grid": p}, device_id_type=MESH)
        rc.start()
        sent.append(rc)
        return rc

    def pot(off):
        return jnp.dot(grad[...], ao[:, pl.ds(pl.multiple_of(off, eighth), quarter)], preferred_element_type=f32)

    def part(b):
        return pl.ds(pl.multiple_of(b * eighth, eighth), eighth)

    def entry_of(f2, f3):
        return h * 4 + lax.rem(b2 + f2, 2) * 2 + lax.rem(b3 + f3, 2)

    def write(e, r):
        out[r, part(e)] = gath[e, r].astype(f32)

    def share(e, r, p):
        return send(gath.at[e, r], gath.at[e, r], p)

    for t in (*range(EARLY, groups - 1), *range(EARLY), groups - 1):
        for k in range(1, AO):
            (gather_copy(t, k) if t < EARLY else whole_copy(t, k)).wait_recv()
        if t < EARLY:
            orot[t, 0:act, :] = jnp.concatenate([orb[t, r] for r in range(AO)], axis=1)
        else:
            w = whole.at[t - EARLY]
            orot[t, 0:act, :] = (w[0] + w[1]) + (w[2] + w[3])
        prepare(t)
        terms(t)

    own, other = h * half, (1 - h) * half
    c1 = []
    for i, b in ((0, 1 - b3), (1, b3)):
        s1_send[i] = pot(other + b * quarter)
        for f in (1 - b2, b2):
            c1.append(send(s1_send.at[i, :, part(f)], s1_recv.at[i, :, part(f)], p1))
    keep[0] = pot(own + (1 - b2) * quarter)
    c2 = []
    for i, b in ((0, 1 - b3), (1, b3)):
        c1[i].wait_recv()
        for r in cuts:
            s2_send[i, r] = (keep[0, r, part(b)] + s1_recv[0, r, part(b)]).astype(bf16)
            c2.append(send(s2_send.at[i, r], s2_recv.at[i, r], p2))
    keep[1] = pot(own + b2 * quarter)
    for i in range(2):
        c1[2 + i].wait_recv()
    keep[1] += s1_recv[1]
    c3 = []
    for k, r in enumerate(cuts):
        c2[k].wait_recv()
        s3_send[r] = (keep[1, r, part(1 - b3)] + s2_recv[0, r].astype(f32)).astype(bf16)
        c3.append(send(s3_send.at[r], s3_recv.at[r], p3))
    g1, g2, g3 = {}, {}, {}
    for k, r in enumerate(cuts):
        c2[CUT + k].wait_recv()
        c3[k].wait_recv()
        e = entry_of(0, 0)
        gath[e, r] = (keep[1, r, part(b3)] + s2_recv[1, r].astype(f32) + s3_recv[r].astype(f32)).astype(bf16)
        g3[k] = share(e, r, p3)
        g2[0, k] = share(e, r, p2)
        g1[0, k] = share(e, r, p1)
        write(e, r)
    for k, r in enumerate(cuts):
        g3[k].wait_recv()
        e = entry_of(0, 1)
        g2[1, k] = share(e, r, p2)
        g1[1, k] = share(e, r, p1)
        write(e, r)
        g2[0, k].wait_recv()
        e = entry_of(1, 0)
        g1[2, k] = share(e, r, p1)
        write(e, r)
    for k, r in enumerate(cuts):
        g2[1, k].wait_recv()
        e = entry_of(1, 1)
        g1[3, k] = share(e, r, p1)
        write(e, r)
    for i, (f2, f3) in enumerate(((0, 0), (0, 1), (1, 0), (1, 1))):
        e = (1 - h) * 4 + lax.rem(b3 + f2, 2) * 2 + lax.rem(b2 + f3, 2)
        for k, r in enumerate(cuts):
            g1[i, k].wait_recv()
            write(e, r)
    for t in range(groups):
        for k in range(1, AO):
            if t < EARLY:
                scatter_copy(t, k).wait_send()
                gather_copy(t, k).wait_send()
            else:
                whole_copy(t, k).wait_send()
    for rc in sent:
        rc.wait_send()


def local_kernel(ao_values, coeffs, screen, core_density, grid_weights, density_matrix, pair_matrix):
    points, cols = ao_values.shape
    states, act = density_matrix.shape[0], density_matrix.shape[1]
    rows, pairs = states * act, act * act
    quarter, eighth = cols // 4, cols // 8
    blocks, wide = points // BLK, AO * BLK
    groups = points // wide
    packed = (act // 2 + 1) * act
    dma, V = pltpu.SemaphoreType.DMA, pltpu.VMEM
    args = (ao_values, coeffs.T, screen, core_density, grid_weights, density_matrix.reshape(rows, act), pair_matrix)
    return pl.pallas_call(
        kernel,
        out_shape=jax.ShapeDtypeStruct((rows, cols), f32),
        in_specs=[pl.BlockSpec(memory_space=pltpu.HBM)] * len(args),
        out_specs=pl.BlockSpec(memory_space=pltpu.VMEM),
        scratch_shapes=[
            V((points, cols), bf16), V((act, cols), bf16), V(screen.shape, jnp.int32), V((points,), f32), V((points,), f32),
            V((rows, act), f32), V(pair_matrix.shape, bf16), V((blocks, act, cols), bf16), V((blocks * act, cols), bf16),
            V((states, packed, 2 * pairs), bf16), V((groups, 2 * pairs, wide), bf16),
            V((groups, packed, wide), f32), V((groups, packed, wide), f32), V((rows, 6 * act), bf16), V((groups, rows, wide), f32),
            V((rows, wide), f32), V((states, wide), f32), V((states, wide), f32), V((rows, points), bf16),
            V((EARLY, AO, act, BLK), f32), V((EARLY, AO - 1, act, BLK), f32), V((EARLY, AO, act, BLK), f32),
            V((groups - EARLY, AO, act, wide), f32),
            V((2, rows, quarter), f32), V((2, rows, quarter), f32),
            V((2, rows, eighth), bf16), V((2, rows, eighth), bf16), V((rows, eighth), bf16), V((rows, eighth), bf16),
            V((2, rows, quarter), f32), V((8, rows, eighth), bf16),
            dma((6 + points // (2 * BLK),)), dma((groups, AO - 1)), dma((groups, AO - 1)),
            dma((groups, AO - 1)), dma((groups, AO - 1)), dma((64,)), dma((64,)),
        ],
        compiler_params=pltpu.CompilerParams(
            collective_id=0, has_side_effects=True, vmem_limit_bytes=46 * 2**20),
    )(*[pltpu.with_memory_space_constraint(v, pltpu.HBM) for v in args])


def solution(mesh):
    fits = mesh.shape["grid"] == GRID and mesh.shape["ao"] == AO
    in_specs = (P("grid", "ao"), P("ao", None), P("grid", "ao"), P("grid"), P("grid"), P(), P())
    out_specs = P(None, "ao")
    return jax.shard_map(local_kernel if fits else local, mesh=mesh, in_specs=in_specs, out_specs=out_specs, check_vma=False)
```

```python
import functools

import jax
import jax.numpy as jnp
from jax import lax
from jax.experimental import pallas as pl
from jax.experimental.pallas import tpu as pltpu
from jax.sharding import PartitionSpec as P

slater_coef = 0.9305257363491
highest = lax.Precision.HIGHEST


def mask_values(ao_values, screen):
    grid_count, basis_count = screen.shape
    height = ao_values.shape[0] // grid_count
    width_cols = ao_values.shape[1] // basis_count
    shaped = ao_values.reshape(grid_count, height, basis_count, width_cols)
    return (shaped * screen.astype(jnp.bfloat16)[:, None, :, None]).reshape(ao_values.shape)


def point_terms(orbitals, core_density, grid_weights, density_matrix, pair_matrix):
    point_count, orbital_count = orbitals.shape
    state_count = density_matrix.shape[0]
    pair_count = orbital_count * orbital_count
    pair_values = (
        (orbitals[:, :, None] * orbitals[:, None, :])
        .reshape(point_count, pair_count)
        .astype(jnp.bfloat16)
    )
    pair_image = jnp.dot(pair_values, pair_matrix, preferred_element_type=jnp.float32).reshape(
        point_count, state_count, pair_count
    )
    on_top = jnp.einsum(
        "bk,bsk->bs", pair_values.astype(jnp.float32), pair_image, precision=highest
    )
    density_grad = jnp.einsum("spq,bq->bsp", density_matrix, orbitals, precision=highest)
    density = core_density[:, None] + jnp.einsum(
        "bp,bsp->bs", orbitals, density_grad, precision=highest
    )
    pair_ratio = 4.0 * on_top / (density * density)
    unclamped = jnp.where(pair_ratio < 1.0, 1.0, 0.0).astype(jnp.float32)
    polarize = jnp.sqrt(jnp.clip(1.0 - pair_ratio, 0.0, 1.0))
    upper_root = (1.0 + polarize) ** (1.0 / 3.0)
    lower_root = (1.0 - polarize) ** (1.0 / 3.0)
    enhance = upper_root**4 + lower_root**4
    slope = (
        4.0 / 3.0 / (upper_root * upper_root + upper_root * lower_root + lower_root * lower_root)
    )
    half_cube = (0.5 * density) ** (1.0 / 3.0)
    quartic = half_cube**4
    pot_pair = 4.0 * slater_coef * quartic * slope * unclamped / (density * density)
    pot_density = -(
        2.0 / 3.0
    ) * slater_coef * half_cube * enhance - 8.0 * slater_coef * quartic * slope * unclamped * on_top / (
        density * density * density
    )
    pair_square = pair_image.reshape(point_count, state_count, orbital_count, orbital_count)
    pair_sym = pair_square + jnp.swapaxes(pair_square, 2, 3)
    pair_grad = jnp.einsum("bspq,bq->bsp", pair_sym, orbitals, precision=highest)
    orbital_grad = grid_weights[:, None, None] * (
        pot_density[:, :, None] * density_grad + pot_pair[:, :, None] * pair_grad
    )
    return orbital_grad.reshape(point_count, state_count * orbital_count).astype(jnp.bfloat16)


def blocked_terms(orbitals, core_density, grid_weights, density_matrix, pair_matrix):
    point_count = orbitals.shape[0]
    row_block = 512
    block_count = point_count // row_block
    pieces = (
        orbitals.reshape(block_count, row_block, orbitals.shape[1]),
        core_density.reshape(block_count, row_block),
        grid_weights.reshape(block_count, row_block),
    )
    stacked = lax.map(
        lambda items: point_terms(items[0], items[1], items[2], density_matrix, pair_matrix), pieces
    )
    return stacked.reshape(point_count, stacked.shape[2])


def contract_rows(gradient, values):
    return lax.dot_general(
        gradient, values, (((0,), (0,)), ((), ())), preferred_element_type=jnp.float32
    )


def local(ao_values, coeffs, screen, core_density, grid_weights, density_matrix, pair_matrix):
    masked = mask_values(ao_values, screen)
    orbitals = lax.psum(jnp.dot(masked, coeffs, preferred_element_type=jnp.float32), "ao")
    gradient = blocked_terms(orbitals, core_density, grid_weights, density_matrix, pair_matrix)
    partial_pot = contract_rows(gradient, masked)
    return lax.psum(partial_pot, "grid")


bf16, f32 = jnp.bfloat16, jnp.float32
MESH = pl.DeviceIdType.MESH
AO, GRID = 4, 8
BLK = 128
CUT, DIRECT = 4, 1


def parts3(v):
    a = v.astype(bf16)
    r = v - a.astype(f32)
    b = r.astype(bf16)
    return a, b, (r - b.astype(f32)).astype(bf16)


def pair_row(index, act):
    first = index % act
    second = (first + index // act) % act
    return first * act + second, second * act + first


def ones_where(cond):
    return jnp.where(cond, 1.0, 0.0)


def kernel(ao_hbm, cf_hbm, screen_hbm, core_hbm, weights_hbm, dens_hbm, pair_hbm, out,
           ao, coeffs, screen, core_den, weights, dens, pair, mask, mcf, mat, pv, pvf, orot, dmat, dg,
           tgrad, top, den, grad, whole, s1_send, s1_recv, s2_send, s2_recv, s3_send, s3_recv,
           keep, gath, ld_sem, z_ss, z_rs, x_ss, x_rs):
    points, cols = ao.shape
    act = whole.shape[2]
    shifts = act // 2 + 1
    packed = shifts * act
    rows = dens.shape[0]
    states = rows // act
    pairs = act * act
    wide = AO * BLK
    groups = points // wide
    half, quarter, eighth = cols // 2, cols // 4, cols // 8
    za = lax.axis_index("ao")
    g = lax.axis_index("grid")
    core, x, y = lax.rem(g, 2), lax.rem(g // 2, 2), g // 4
    h = lax.rem(core + x + y, 2)
    b2 = x * (1 - h) + y * h
    b3 = y * (1 - h) + x * h
    p1 = g + 1 - 2 * core
    p2 = p1 + (1 - h) * (2 - 4 * x) + h * (4 - 8 * y)
    p3 = p1 + h * (2 - 4 * x) + (1 - h) * (4 - 8 * y)

    barrier = pltpu.get_barrier_semaphore()
    for k in range(1, AO):
        pl.semaphore_signal(barrier, inc=1, device_id={"ao": lax.rem(za + k, AO)}, device_id_type=MESH)
    p23 = g + 2 - 4 * x + 4 - 8 * y
    for p in (p1, p2, p3, p23):
        pl.semaphore_signal(barrier, inc=1, device_id={"grid": p}, device_id_type=MESH)

    def load(src, dst, i):
        cp = pltpu.make_async_copy(src, dst, ld_sem.at[i])
        cp.start()
        return cp

    step = 2 * BLK
    small = [load(s, d, i) for i, (s, d) in enumerate(((cf_hbm, coeffs), (screen_hbm, screen)))]
    loads = [load(ao_hbm.at[pl.ds(i * step, step)], ao.at[pl.ds(i * step, step)], 2 + i) for i in range(points // step)]
    late = [load(s, d, 2 + len(loads) + i) for i, (s, d) in enumerate(
        ((pair_hbm, pair), (dens_hbm, dens), (core_hbm, core_den), (weights_hbm, weights)))]

    for cp in small:
        cp.wait()
    cf = coeffs[...]
    marks = screen[...].astype(f32)
    for j in range(cols // BLK):
        v = jnp.broadcast_to(marks[:, j:j + 1], (points // BLK, BLK))
        for i in range(points // BLK):
            mask[i, :, j * BLK:(j + 1) * BLK] = jnp.broadcast_to(v[i:i + 1, :], (act, BLK)).astype(bf16)
    for i in range(points // BLK):
        mcf[i * act:(i + 1) * act, :] = cf * mask[i]

    def z_copy(src, dst, ss, rs, t, k):
        return pltpu.make_async_remote_copy(
            src_ref=src, dst_ref=dst, send_sem=ss.at[t, k - 1], recv_sem=rs.at[t, k - 1],
            device_id={"ao": lax.rem(za + k, AO)}, device_id_type=MESH)

    def whole_copy(t, k):
        return z_copy(whole.at[t, za], whole.at[t, za], z_ss, z_rs, t, k)

    for t in range(groups):
        for u in range(2):
            i = 2 * t + u
            loads[i].wait()
            r = lax.dot_general(mcf[2 * i * act:2 * (i + 1) * act, :], ao[i * step:(i + 1) * step, :],
                                (((1,), (1,)), ((), ())), preferred_element_type=f32)
            whole[t, za, :, u * step:u * step + BLK] = r[0:act, 0:BLK]
            whole[t, za, :, u * step + BLK:(u + 1) * step] = r[act:, BLK:]
        if t == 0:
            pl.semaphore_wait(barrier, AO - 1 + 4)
        for k in range(1, AO):
            whole_copy(t, k).start()

    for cp in late:
        cp.wait()
    d1, d2, d3 = parts3(dens[...])
    dmat[...] = jnp.concatenate([v.astype(f32) for v in (d1, d1, d2, d2, d1, d3)], axis=1).astype(bf16)
    fp, fq = pair_row(lax.broadcasted_iota(jnp.int32, (packed, pairs), 0), act)
    ci = lax.broadcasted_iota(jnp.int32, (packed, pairs), 1)
    fold_rows = (ones_where(ci == fp) + ones_where(ci == fq)).astype(bf16)
    few = 3
    for b in range(states // few):
        folded = jnp.dot(fold_rows, pair[:, b * few * pairs:(b + 1) * few * pairs], preferred_element_type=f32)
        hi = folded.astype(bf16)
        lo = (folded - hi.astype(f32)).astype(bf16)
        for i in range(few):
            mat[b * few + i, :, 0:pairs] = hi[:, i * pairs:(i + 1) * pairs]
            mat[b * few + i, :, pairs:] = lo[:, i * pairs:(i + 1) * pairs]

    def screen_rows(i, c):
        at = pl.multiple_of(i * BLK, BLK)
        for j in range(cols // BLK):
            m = jnp.concatenate([mask[i, :, j * BLK:(j + 1) * BLK]] * (BLK // mask.shape[1]), axis=0)
            ao[pl.ds(at, BLK), j * BLK:(j + 1) * BLK] = ao[pl.ds(at, BLK), j * BLK:(j + 1) * BLK] * m
        return c

    lax.fori_loop(0, points // BLK, screen_rows, 0)

    def prepare(t):
        o = orot[t, 0:act, :]
        for d in range(shifts):
            od = o if d == 0 else jnp.concatenate([o[d:], o[:d]], axis=0)
            if d:
                orot[t, d * act:(d + 1) * act, :] = od
            v = (o * od).astype(bf16)
            edge = d == 0 or d == shifts - 1
            pvf[t, d * act:(d + 1) * act, :] = v.astype(f32) * (0.5 if edge else 1.0)
        for p in range(act):
            v = (o[p:p + 1, :] * o).astype(bf16)
            pv[t, p * act:(p + 1) * act, :] = v
            pv[t, pairs + p * act:pairs + (p + 1) * act, :] = v
        o1, o2, o3 = parts3(o)
        dg[t] = jnp.dot(dmat[...], jnp.concatenate([o1, o2, o1, o2, o3, o1], axis=0), preferred_element_type=f32)

    def terms(t):
        o = orot[t, 0:act, :]
        image = jnp.dot(mat[...].reshape(states * packed, mat.shape[2]), pv[t], preferred_element_type=f32)
        for s in range(states):
            z = [image[s * packed + d * act:s * packed + (d + 1) * act, :] for d in range(shifts)]
            ot = z[0] * pvf[t, 0:act, :]
            tg = z[0] * o
            for d in range(1, shifts):
                ot = ot + z[d] * pvf[t, d * act:(d + 1) * act, :]
                tg = tg + z[d] * orot[t, d * act:(d + 1) * act, :]
            back = z[shifts - 2] * o
            for d in range(shifts - 3, -1, -1):
                back = jnp.concatenate([back[act - 1:], back[:act - 1]], axis=0)
                if d:
                    back = back + z[d] * o
            at = s * act
            tgrad[at:at + act, :] = tg + back
            top[s:s + 1, :] = jnp.sum(ot, axis=0, keepdims=True)
            den[s:s + 1, :] = jnp.sum(o * dg[t, at:at + act, :], axis=0, keepdims=True)
        start = pl.multiple_of(t * wide, wide)
        third = 1.0 / 3.0
        on_top = top[...]
        density = core_den[pl.ds(start, wide)].reshape(1, wide) + den[...]
        ratio = 4.0 * on_top / (density * density)
        unclamped = jnp.where(ratio < 1.0, 1.0, 0.0)
        polarize = jnp.sqrt(jnp.minimum(jnp.maximum(1.0 - ratio, 0.0), 1.0))
        upper = jnp.exp(jnp.log(1.0 + polarize) * third)
        lower = jnp.exp(jnp.log(1.0 - polarize) * third)
        u2, l2 = upper * upper, lower * lower
        enhance = u2 * u2 + l2 * l2
        slope = 4.0 / 3.0 / (u2 + upper * lower + l2)
        hc = jnp.exp(jnp.log(0.5 * density) * third)
        h2 = hc * hc
        base = 4.0 * slater_coef * (h2 * h2) * slope * unclamped / (density * density)
        pot_den = -(2.0 / 3.0) * slater_coef * hc * enhance - 2.0 * base * on_top / density
        w = weights[pl.ds(start, wide)].reshape(1, wide)
        top[...] = base * w
        den[...] = pot_den * w
        for s in range(states):
            at = s * act
            grad[at:at + act, pl.ds(start, wide)] = (
                den[s:s + 1, :] * dg[t, at:at + act, :] + top[s:s + 1, :] * tgrad[at:at + act, :]
            ).astype(bf16)

    cut = rows // CUT
    cuts = [slice(k * cut, (k + 1) * cut) for k in range(CUT)]
    sent = []

    def send(src, dst, p):
        i = len(sent)
        rc = pltpu.make_async_remote_copy(
            src_ref=src, dst_ref=dst, send_sem=x_ss.at[i], recv_sem=x_rs.at[i], device_id={"grid": p}, device_id_type=MESH)
        rc.start()
        sent.append(rc)
        return rc

    def pot(off):
        return jnp.dot(grad[...], ao[:, pl.ds(pl.multiple_of(off, eighth), quarter)], preferred_element_type=f32)

    def part(b):
        return pl.ds(pl.multiple_of(b * eighth, eighth), eighth)

    def entry_of(f2, f3):
        return h * 4 + lax.rem(b2 + f2, 2) * 2 + lax.rem(b3 + f3, 2)

    def write(e, r):
        out[r, part(e)] = gath[e, r].astype(f32)

    def share(e, r, p):
        return send(gath.at[e, r], gath.at[e, r], p)

    for t in range(groups):
        for k in range(1, AO):
            whole_copy(t, k).wait_recv()
        w = whole.at[t]
        orot[t, 0:act, :] = (w[0] + w[1]) + (w[2] + w[3])
        prepare(t)
        terms(t)

    own, other = h * half, (1 - h) * half
    c1, c2 = [], []

    def give(i, b):
        s1_send[i] = pot(other + b * quarter)
        for f in (1 - b2, b2):
            c1.append(send(s1_send.at[i, :, part(f)], s1_recv.at[i, :, part(f)], p1))

    give(0, 1 - b3)
    keep[0] = pot(own + (1 - b2) * quarter)
    for i, b in ((0, 1 - b3), (1, b3)):
        c1[i].wait_recv()
        for r in cuts:
            s2_send[i, r] = (keep[0, r, part(b)] + s1_recv[0, r, part(b)]).astype(bf16)
            c2.append(send(s2_send.at[i, r], s2_recv.at[i, r], p2))
    give(1, b3)
    keep[1] = pot(own + b2 * quarter)
    for i in range(2):
        c1[2 + i].wait_recv()
    keep[1] += s1_recv[1]
    c3 = []
    for k, r in enumerate(cuts):
        c2[k].wait_recv()
        s3_send[r] = (keep[1, r, part(1 - b3)] + s2_recv[0, r].astype(f32)).astype(bf16)
        c3.append(send(s3_send.at[r], s3_recv.at[r], p3))
    g1, g2, g3 = {}, {}, {}
    for k, r in enumerate(cuts):
        c2[CUT + k].wait_recv()
        c3[k].wait_recv()
        e = entry_of(0, 0)
        gath[e, r] = (keep[1, r, part(b3)] + s2_recv[1, r].astype(f32) + s3_recv[r].astype(f32)).astype(bf16)
        g3[k] = share(e, r, p3)
        g2[0, k] = share(e, r, p2)
        if k >= CUT - DIRECT:
            g2[1, k] = share(e, r, p23)
        g1[0, k] = share(e, r, p1)
        write(e, r)
    for k, r in enumerate(cuts):
        g3[k].wait_recv()
        e = entry_of(0, 1)
        if k < CUT - DIRECT:
            g2[1, k] = share(e, r, p2)
        g1[1, k] = share(e, r, p1)
        write(e, r)
        g2[0, k].wait_recv()
        e = entry_of(1, 0)
        g1[2, k] = share(e, r, p1)
        write(e, r)
    for k, r in enumerate(cuts):
        g2[1, k].wait_recv()
        e = entry_of(1, 1)
        g1[3, k] = share(e, r, p1)
        write(e, r)
    for i, (f2, f3) in enumerate(((0, 0), (0, 1), (1, 0), (1, 1))):
        e = (1 - h) * 4 + lax.rem(b3 + f2, 2) * 2 + lax.rem(b2 + f3, 2)
        for k, r in enumerate(cuts):
            g1[i, k].wait_recv()
            write(e, r)
    for t in range(groups):
        for k in range(1, AO):
            whole_copy(t, k).wait_send()
    for rc in sent:
        rc.wait_send()


def local_kernel(ao_values, coeffs, screen, core_density, grid_weights, density_matrix, pair_matrix):
    points, cols = ao_values.shape
    states, act = density_matrix.shape[0], density_matrix.shape[1]
    rows, pairs = states * act, act * act
    quarter, eighth = cols // 4, cols // 8
    blocks, wide = points // BLK, AO * BLK
    groups = points // wide
    packed = (act // 2 + 1) * act
    dma, V = pltpu.SemaphoreType.DMA, pltpu.VMEM
    args = (ao_values, coeffs.T, screen, core_density, grid_weights, density_matrix.reshape(rows, act), pair_matrix)
    return pl.pallas_call(
        kernel,
        out_shape=jax.ShapeDtypeStruct((rows, cols), f32),
        in_specs=[pl.BlockSpec(memory_space=pltpu.HBM)] * len(args),
        out_specs=pl.BlockSpec(memory_space=pltpu.VMEM),
        scratch_shapes=[
            V((points, cols), bf16), V((act, cols), bf16), V(screen.shape, jnp.int32), V((points,), f32), V((points,), f32),
            V((rows, act), f32), V(pair_matrix.shape, bf16), V((blocks, act, cols), bf16), V((blocks * act, cols), bf16),
            V((states, packed, 2 * pairs), bf16), V((groups, 2 * pairs, wide), bf16),
            V((groups, packed, wide), f32), V((groups, packed, wide), f32), V((rows, 6 * act), bf16), V((groups, rows, wide), f32),
            V((rows, wide), f32), V((states, wide), f32), V((states, wide), f32), V((rows, points), bf16),
            V((groups, AO, act, wide), f32),
            V((2, rows, quarter), f32), V((2, rows, quarter), f32),
            V((2, rows, eighth), bf16), V((2, rows, eighth), bf16), V((rows, eighth), bf16), V((rows, eighth), bf16),
            V((2, rows, quarter), f32), V((8, rows, eighth), bf16),
            dma((6 + points // (2 * BLK),)), dma((groups, AO - 1)), dma((groups, AO - 1)), dma((64,)), dma((64,)),
        ],
        compiler_params=pltpu.CompilerParams(
            collective_id=0, has_side_effects=True, vmem_limit_bytes=46 * 2**20),
    )(*[pltpu.with_memory_space_constraint(v, pltpu.HBM) for v in args])


def solution(mesh):
    fits = mesh.shape["grid"] == GRID and mesh.shape["ao"] == AO
    in_specs = (P("grid", "ao"), P("ao", None), P("grid", "ao"), P("grid"), P("grid"), P(), P())
    out_specs = P(None, "ao")
    return jax.shard_map(local_kernel if fits else local, mesh=mesh, in_specs=in_specs, out_specs=out_specs, check_vma=False)
```

```python
import functools

import jax
import jax.numpy as jnp
from jax import lax
from jax.experimental import pallas as pl
from jax.experimental.pallas import tpu as pltpu
from jax.sharding import PartitionSpec as P

slater_coef = 0.9305257363491
highest = lax.Precision.HIGHEST


def mask_values(ao_values, screen):
    grid_count, basis_count = screen.shape
    height = ao_values.shape[0] // grid_count
    width_cols = ao_values.shape[1] // basis_count
    shaped = ao_values.reshape(grid_count, height, basis_count, width_cols)
    return (shaped * screen.astype(jnp.bfloat16)[:, None, :, None]).reshape(ao_values.shape)


def point_terms(orbitals, core_density, grid_weights, density_matrix, pair_matrix):
    point_count, orbital_count = orbitals.shape
    state_count = density_matrix.shape[0]
    pair_count = orbital_count * orbital_count
    pair_values = (
        (orbitals[:, :, None] * orbitals[:, None, :])
        .reshape(point_count, pair_count)
        .astype(jnp.bfloat16)
    )
    pair_image = jnp.dot(pair_values, pair_matrix, preferred_element_type=jnp.float32).reshape(
        point_count, state_count, pair_count
    )
    on_top = jnp.einsum(
        "bk,bsk->bs", pair_values.astype(jnp.float32), pair_image, precision=highest
    )
    density_grad = jnp.einsum("spq,bq->bsp", density_matrix, orbitals, precision=highest)
    density = core_density[:, None] + jnp.einsum(
        "bp,bsp->bs", orbitals, density_grad, precision=highest
    )
    pair_ratio = 4.0 * on_top / (density * density)
    unclamped = jnp.where(pair_ratio < 1.0, 1.0, 0.0).astype(jnp.float32)
    polarize = jnp.sqrt(jnp.clip(1.0 - pair_ratio, 0.0, 1.0))
    upper_root = (1.0 + polarize) ** (1.0 / 3.0)
    lower_root = (1.0 - polarize) ** (1.0 / 3.0)
    enhance = upper_root**4 + lower_root**4
    slope = (
        4.0 / 3.0 / (upper_root * upper_root + upper_root * lower_root + lower_root * lower_root)
    )
    half_cube = (0.5 * density) ** (1.0 / 3.0)
    quartic = half_cube**4
    pot_pair = 4.0 * slater_coef * quartic * slope * unclamped / (density * density)
    pot_density = -(
        2.0 / 3.0
    ) * slater_coef * half_cube * enhance - 8.0 * slater_coef * quartic * slope * unclamped * on_top / (
        density * density * density
    )
    pair_square = pair_image.reshape(point_count, state_count, orbital_count, orbital_count)
    pair_sym = pair_square + jnp.swapaxes(pair_square, 2, 3)
    pair_grad = jnp.einsum("bspq,bq->bsp", pair_sym, orbitals, precision=highest)
    orbital_grad = grid_weights[:, None, None] * (
        pot_density[:, :, None] * density_grad + pot_pair[:, :, None] * pair_grad
    )
    return orbital_grad.reshape(point_count, state_count * orbital_count).astype(jnp.bfloat16)


def blocked_terms(orbitals, core_density, grid_weights, density_matrix, pair_matrix):
    point_count = orbitals.shape[0]
    row_block = 512
    block_count = point_count // row_block
    pieces = (
        orbitals.reshape(block_count, row_block, orbitals.shape[1]),
        core_density.reshape(block_count, row_block),
        grid_weights.reshape(block_count, row_block),
    )
    stacked = lax.map(
        lambda items: point_terms(items[0], items[1], items[2], density_matrix, pair_matrix), pieces
    )
    return stacked.reshape(point_count, stacked.shape[2])


def contract_rows(gradient, values):
    return lax.dot_general(
        gradient, values, (((0,), (0,)), ((), ())), preferred_element_type=jnp.float32
    )


def local(ao_values, coeffs, screen, core_density, grid_weights, density_matrix, pair_matrix):
    masked = mask_values(ao_values, screen)
    orbitals = lax.psum(jnp.dot(masked, coeffs, preferred_element_type=jnp.float32), "ao")
    gradient = blocked_terms(orbitals, core_density, grid_weights, density_matrix, pair_matrix)
    partial_pot = contract_rows(gradient, masked)
    return lax.psum(partial_pot, "grid")


bf16, f32 = jnp.bfloat16, jnp.float32
MESH = pl.DeviceIdType.MESH
AO, GRID = 4, 8
BLK = 128
CUT, DIRECT = 4, 0


def parts3(v):
    a = v.astype(bf16)
    r = v - a.astype(f32)
    b = r.astype(bf16)
    return a, b, (r - b.astype(f32)).astype(bf16)


def pair_row(index, act):
    first = index % act
    second = (first + index // act) % act
    return first * act + second, second * act + first


def ones_where(cond):
    return jnp.where(cond, 1.0, 0.0)


def kernel(ao_hbm, cf_hbm, screen_hbm, core_hbm, weights_hbm, dens_hbm, pair_hbm, out,
           ao, coeffs, screen, core_den, weights, dens, pair, mask, mcf, mat, pv, pvf, orot, dmat, dg,
           tgrad, top, den, grad, whole, s1_send, s1_recv, s2_send, s2_recv, s3_send, s3_recv,
           keep, gath, ld_sem, z_ss, z_rs, x_ss, x_rs):
    points, cols = ao.shape
    act = whole.shape[2]
    shifts = act // 2 + 1
    packed = shifts * act
    rows = dens.shape[0]
    states = rows // act
    pairs = act * act
    wide = AO * BLK
    groups = points // wide
    half, quarter, eighth = cols // 2, cols // 4, cols // 8
    za = lax.axis_index("ao")
    g = lax.axis_index("grid")
    core, x, y = lax.rem(g, 2), lax.rem(g // 2, 2), g // 4
    h = lax.rem(core + x + y, 2)
    b2 = x * (1 - h) + y * h
    b3 = y * (1 - h) + x * h
    p1 = g + 1 - 2 * core
    p2 = p1 + (1 - h) * (2 - 4 * x) + h * (4 - 8 * y)
    p3 = p1 + h * (2 - 4 * x) + (1 - h) * (4 - 8 * y)

    barrier = pltpu.get_barrier_semaphore()
    for k in range(1, AO):
        pl.semaphore_signal(barrier, inc=1, device_id={"ao": lax.rem(za + k, AO)}, device_id_type=MESH)
    p23 = g + 2 - 4 * x + 4 - 8 * y
    for p in (p1, p2, p3, p23):
        pl.semaphore_signal(barrier, inc=1, device_id={"grid": p}, device_id_type=MESH)

    def load(src, dst, i):
        cp = pltpu.make_async_copy(src, dst, ld_sem.at[i])
        cp.start()
        return cp

    step = 2 * BLK
    small = [load(s, d, i) for i, (s, d) in enumerate(((cf_hbm, coeffs), (screen_hbm, screen)))]
    loads = [load(ao_hbm.at[pl.ds(i * step, step)], ao.at[pl.ds(i * step, step)], 2 + i) for i in range(points // step)]
    late = [load(s, d, 2 + len(loads) + i) for i, (s, d) in enumerate(
        ((pair_hbm, pair), (dens_hbm, dens), (core_hbm, core_den), (weights_hbm, weights)))]

    for cp in small:
        cp.wait()
    cf = coeffs[...]
    marks = screen[...].astype(f32)
    for j in range(cols // BLK):
        v = jnp.broadcast_to(marks[:, j:j + 1], (points // BLK, BLK))
        for i in range(points // BLK):
            mask[i, :, j * BLK:(j + 1) * BLK] = jnp.broadcast_to(v[i:i + 1, :], (act, BLK)).astype(bf16)
    for i in range(points // BLK):
        mcf[i * act:(i + 1) * act, :] = cf * mask[i]

    def z_copy(src, dst, ss, rs, t, k):
        return pltpu.make_async_remote_copy(
            src_ref=src, dst_ref=dst, send_sem=ss.at[t, k - 1], recv_sem=rs.at[t, k - 1],
            device_id={"ao": lax.rem(za + k, AO)}, device_id_type=MESH)

    def whole_copy(t, k):
        return z_copy(whole.at[t, za], whole.at[t, za], z_ss, z_rs, t, k)

    for t in range(groups):
        for u in range(2):
            i = 2 * t + u
            loads[i].wait()
            r = lax.dot_general(mcf[2 * i * act:2 * (i + 1) * act, :], ao[i * step:(i + 1) * step, :],
                                (((1,), (1,)), ((), ())), preferred_element_type=f32)
            whole[t, za, :, u * step:u * step + BLK] = r[0:act, 0:BLK]
            whole[t, za, :, u * step + BLK:(u + 1) * step] = r[act:, BLK:]
        if t == 0:
            pl.semaphore_wait(barrier, AO - 1 + 4)
        for k in range(1, AO):
            whole_copy(t, k).start()

    for cp in late:
        cp.wait()
    d1, d2, d3 = parts3(dens[...])
    dmat[...] = jnp.concatenate([v.astype(f32) for v in (d1, d1, d2, d2, d1, d3)], axis=1).astype(bf16)
    fp, fq = pair_row(lax.broadcasted_iota(jnp.int32, (packed, pairs), 0), act)
    ci = lax.broadcasted_iota(jnp.int32, (packed, pairs), 1)
    fold_rows = (ones_where(ci == fp) + ones_where(ci == fq)).astype(bf16)
    few = 3
    for b in range(states // few):
        folded = jnp.dot(fold_rows, pair[:, b * few * pairs:(b + 1) * few * pairs], preferred_element_type=f32)
        hi = folded.astype(bf16)
        lo = (folded - hi.astype(f32)).astype(bf16)
        for i in range(few):
            mat[b * few + i, :, 0:pairs] = hi[:, i * pairs:(i + 1) * pairs]
            mat[b * few + i, :, pairs:] = lo[:, i * pairs:(i + 1) * pairs]

    def screen_rows(i, c):
        at = pl.multiple_of(i * BLK, BLK)
        for j in range(cols // BLK):
            m = jnp.concatenate([mask[i, :, j * BLK:(j + 1) * BLK]] * (BLK // mask.shape[1]), axis=0)
            ao[pl.ds(at, BLK), j * BLK:(j + 1) * BLK] = ao[pl.ds(at, BLK), j * BLK:(j + 1) * BLK] * m
        return c

    lax.fori_loop(0, points // BLK, screen_rows, 0)

    def prepare(t):
        o = orot[t, 0:act, :]
        for d in range(shifts):
            od = o if d == 0 else jnp.concatenate([o[d:], o[:d]], axis=0)
            if d:
                orot[t, d * act:(d + 1) * act, :] = od
            v = (o * od).astype(bf16)
            edge = d == 0 or d == shifts - 1
            pvf[t, d * act:(d + 1) * act, :] = v.astype(f32) * (0.5 if edge else 1.0)
        for p in range(act):
            v = (o[p:p + 1, :] * o).astype(bf16)
            pv[t, p * act:(p + 1) * act, :] = v
            pv[t, pairs + p * act:pairs + (p + 1) * act, :] = v
        o1, o2, o3 = parts3(o)
        dg[t] = jnp.dot(dmat[...], jnp.concatenate([o1, o2, o1, o2, o3, o1], axis=0), preferred_element_type=f32)

    def terms(t):
        o = orot[t, 0:act, :]
        image = jnp.dot(mat[...].reshape(states * packed, mat.shape[2]), pv[t], preferred_element_type=f32)
        for s in range(states):
            z = [image[s * packed + d * act:s * packed + (d + 1) * act, :] for d in range(shifts)]
            ot = z[0] * pvf[t, 0:act, :]
            tg = z[0] * o
            for d in range(1, shifts):
                ot = ot + z[d] * pvf[t, d * act:(d + 1) * act, :]
                tg = tg + z[d] * orot[t, d * act:(d + 1) * act, :]
            back = z[shifts - 2] * o
            for d in range(shifts - 3, -1, -1):
                back = jnp.concatenate([back[act - 1:], back[:act - 1]], axis=0)
                if d:
                    back = back + z[d] * o
            at = s * act
            tgrad[at:at + act, :] = tg + back
            top[s:s + 1, :] = jnp.sum(ot, axis=0, keepdims=True)
            den[s:s + 1, :] = jnp.sum(o * dg[t, at:at + act, :], axis=0, keepdims=True)
        start = pl.multiple_of(t * wide, wide)
        third = 1.0 / 3.0
        on_top = top[...]
        density = core_den[pl.ds(start, wide)].reshape(1, wide) + den[...]
        ratio = 4.0 * on_top / (density * density)
        unclamped = jnp.where(ratio < 1.0, 1.0, 0.0)
        polarize = jnp.sqrt(jnp.minimum(jnp.maximum(1.0 - ratio, 0.0), 1.0))
        upper = jnp.exp(jnp.log(1.0 + polarize) * third)
        lower = jnp.exp(jnp.log(1.0 - polarize) * third)
        u2, l2 = upper * upper, lower * lower
        enhance = u2 * u2 + l2 * l2
        slope = 4.0 / 3.0 / (u2 + upper * lower + l2)
        hc = jnp.exp(jnp.log(0.5 * density) * third)
        h2 = hc * hc
        base = 4.0 * slater_coef * (h2 * h2) * slope * unclamped / (density * density)
        pot_den = -(2.0 / 3.0) * slater_coef * hc * enhance - 2.0 * base * on_top / density
        w = weights[pl.ds(start, wide)].reshape(1, wide)
        top[...] = base * w
        den[...] = pot_den * w
        for s in range(states):
            at = s * act
            grad[at:at + act, pl.ds(start, wide)] = (
                den[s:s + 1, :] * dg[t, at:at + act, :] + top[s:s + 1, :] * tgrad[at:at + act, :]
            ).astype(bf16)

    cut = rows // CUT
    cuts = [slice(k * cut, (k + 1) * cut) for k in range(CUT)]
    sent = []

    def send(src, dst, p):
        i = len(sent)
        rc = pltpu.make_async_remote_copy(
            src_ref=src, dst_ref=dst, send_sem=x_ss.at[i], recv_sem=x_rs.at[i], device_id={"grid": p}, device_id_type=MESH)
        rc.start()
        sent.append(rc)
        return rc

    def pot(off):
        return jnp.dot(grad[...], ao[:, pl.ds(pl.multiple_of(off, eighth), quarter)], preferred_element_type=f32)

    def part(b):
        return pl.ds(pl.multiple_of(b * eighth, eighth), eighth)

    def entry_of(f2, f3):
        return h * 4 + lax.rem(b2 + f2, 2) * 2 + lax.rem(b3 + f3, 2)

    def write(e, r):
        out[r, part(e)] = gath[e, r].astype(f32)

    def share(e, r, p):
        return send(gath.at[e, r], gath.at[e, r], p)

    for t in range(groups):
        for k in range(1, AO):
            whole_copy(t, k).wait_recv()
        w = whole.at[t]
        orot[t, 0:act, :] = (w[0] + w[1]) + (w[2] + w[3])
        prepare(t)
        terms(t)

    own, other = h * half, (1 - h) * half
    c1, c2 = [], []

    def give(i, b):
        s1_send[i] = pot(other + b * quarter)
        for f in (1 - b2, b2):
            c1.append(send(s1_send.at[i, :, part(f)], s1_recv.at[i, :, part(f)], p1))

    give(0, 1 - b3)
    keep[0] = pot(own + (1 - b2) * quarter)
    for i, b in ((0, 1 - b3), (1, b3)):
        c1[i].wait_recv()
        for r in cuts:
            s2_send[i, r] = (keep[0, r, part(b)] + s1_recv[0, r, part(b)]).astype(bf16)
            c2.append(send(s2_send.at[i, r], s2_recv.at[i, r], p2))
    give(1, b3)
    keep[1] = pot(own + b2 * quarter)
    for i in range(2):
        c1[2 + i].wait_recv()
    keep[1] += s1_recv[1]
    c3 = []
    for k, r in enumerate(cuts):
        c2[k].wait_recv()
        s3_send[r] = (keep[1, r, part(1 - b3)] + s2_recv[0, r].astype(f32)).astype(bf16)
        c3.append(send(s3_send.at[r], s3_recv.at[r], p3))
    g1, g2, g3 = {}, {}, {}
    for k, r in enumerate(cuts):
        c2[CUT + k].wait_recv()
        c3[k].wait_recv()
        e = entry_of(0, 0)
        gath[e, r] = (keep[1, r, part(b3)] + s2_recv[1, r].astype(f32) + s3_recv[r].astype(f32)).astype(bf16)
        g3[k] = share(e, r, p3)
        if k >= CUT - DIRECT:
            g2[1, k] = share(e, r, p23)
        g1[0, k] = share(e, r, p1)
    for k, r in enumerate(cuts):
        e = entry_of(0, 0)
        g2[0, k] = share(e, r, p2)
        write(e, r)
    for k, r in enumerate(cuts):
        g3[k].wait_recv()
        e = entry_of(0, 1)
        if k < CUT - DIRECT:
            g2[1, k] = share(e, r, p2)
        g1[1, k] = share(e, r, p1)
        write(e, r)
    for k, r in enumerate(cuts):
        g2[0, k].wait_recv()
        e = entry_of(1, 0)
        g1[2, k] = share(e, r, p1)
        write(e, r)
    for k, r in enumerate(cuts):
        g2[1, k].wait_recv()
        e = entry_of(1, 1)
        g1[3, k] = share(e, r, p1)
        write(e, r)
    for i, (f2, f3) in enumerate(((0, 0), (0, 1), (1, 0), (1, 1))):
        e = (1 - h) * 4 + lax.rem(b3 + f2, 2) * 2 + lax.rem(b2 + f3, 2)
        for k, r in enumerate(cuts):
            g1[i, k].wait_recv()
            write(e, r)
    for t in range(groups):
        for k in range(1, AO):
            whole_copy(t, k).wait_send()
    for rc in sent:
        rc.wait_send()


def local_kernel(ao_values, coeffs, screen, core_density, grid_weights, density_matrix, pair_matrix):
    points, cols = ao_values.shape
    states, act = density_matrix.shape[0], density_matrix.shape[1]
    rows, pairs = states * act, act * act
    quarter, eighth = cols // 4, cols // 8
    blocks, wide = points // BLK, AO * BLK
    groups = points // wide
    packed = (act // 2 + 1) * act
    dma, V = pltpu.SemaphoreType.DMA, pltpu.VMEM
    args = (ao_values, coeffs.T, screen, core_density, grid_weights, density_matrix.reshape(rows, act), pair_matrix)
    return pl.pallas_call(
        kernel,
        out_shape=jax.ShapeDtypeStruct((rows, cols), f32),
        in_specs=[pl.BlockSpec(memory_space=pltpu.HBM)] * len(args),
        out_specs=pl.BlockSpec(memory_space=pltpu.VMEM),
        scratch_shapes=[
            V((points, cols), bf16), V((act, cols), bf16), V(screen.shape, jnp.int32), V((points,), f32), V((points,), f32),
            V((rows, act), f32), V(pair_matrix.shape, bf16), V((blocks, act, cols), bf16), V((blocks * act, cols), bf16),
            V((states, packed, 2 * pairs), bf16), V((groups, 2 * pairs, wide), bf16),
            V((groups, packed, wide), f32), V((groups, packed, wide), f32), V((rows, 6 * act), bf16), V((groups, rows, wide), f32),
            V((rows, wide), f32), V((states, wide), f32), V((states, wide), f32), V((rows, points), bf16),
            V((groups, AO, act, wide), f32),
            V((2, rows, quarter), f32), V((2, rows, quarter), f32),
            V((2, rows, eighth), bf16), V((2, rows, eighth), bf16), V((rows, eighth), bf16), V((rows, eighth), bf16),
            V((2, rows, quarter), f32), V((8, rows, eighth), bf16),
            dma((6 + points // (2 * BLK),)), dma((groups, AO - 1)), dma((groups, AO - 1)), dma((64,)), dma((64,)),
        ],
        compiler_params=pltpu.CompilerParams(
            collective_id=0, has_side_effects=True, vmem_limit_bytes=46 * 2**20),
    )(*[pltpu.with_memory_space_constraint(v, pltpu.HBM) for v in args])


def solution(mesh):
    fits = mesh.shape["grid"] == GRID and mesh.shape["ao"] == AO
    in_specs = (P("grid", "ao"), P("ao", None), P("grid", "ao"), P("grid"), P("grid"), P(), P())
    out_specs = P(None, "ao")
    return jax.shard_map(local_kernel if fits else local, mesh=mesh, in_specs=in_specs, out_specs=out_specs, check_vma=False)
```

```python
import functools

import jax
import jax.numpy as jnp
from jax import lax
from jax.experimental import pallas as pl
from jax.experimental.pallas import tpu as pltpu
from jax.sharding import PartitionSpec as P

slater_coef = 0.9305257363491
highest = lax.Precision.HIGHEST


def mask_values(ao_values, screen):
    grid_count, basis_count = screen.shape
    height = ao_values.shape[0] // grid_count
    width_cols = ao_values.shape[1] // basis_count
    shaped = ao_values.reshape(grid_count, height, basis_count, width_cols)
    return (shaped * screen.astype(jnp.bfloat16)[:, None, :, None]).reshape(ao_values.shape)


def point_terms(orbitals, core_density, grid_weights, density_matrix, pair_matrix):
    point_count, orbital_count = orbitals.shape
    state_count = density_matrix.shape[0]
    pair_count = orbital_count * orbital_count
    pair_values = (
        (orbitals[:, :, None] * orbitals[:, None, :])
        .reshape(point_count, pair_count)
        .astype(jnp.bfloat16)
    )
    pair_image = jnp.dot(pair_values, pair_matrix, preferred_element_type=jnp.float32).reshape(
        point_count, state_count, pair_count
    )
    on_top = jnp.einsum(
        "bk,bsk->bs", pair_values.astype(jnp.float32), pair_image, precision=highest
    )
    density_grad = jnp.einsum("spq,bq->bsp", density_matrix, orbitals, precision=highest)
    density = core_density[:, None] + jnp.einsum(
        "bp,bsp->bs", orbitals, density_grad, precision=highest
    )
    pair_ratio = 4.0 * on_top / (density * density)
    unclamped = jnp.where(pair_ratio < 1.0, 1.0, 0.0).astype(jnp.float32)
    polarize = jnp.sqrt(jnp.clip(1.0 - pair_ratio, 0.0, 1.0))
    upper_root = (1.0 + polarize) ** (1.0 / 3.0)
    lower_root = (1.0 - polarize) ** (1.0 / 3.0)
    enhance = upper_root**4 + lower_root**4
    slope = (
        4.0 / 3.0 / (upper_root * upper_root + upper_root * lower_root + lower_root * lower_root)
    )
    half_cube = (0.5 * density) ** (1.0 / 3.0)
    quartic = half_cube**4
    pot_pair = 4.0 * slater_coef * quartic * slope * unclamped / (density * density)
    pot_density = -(
        2.0 / 3.0
    ) * slater_coef * half_cube * enhance - 8.0 * slater_coef * quartic * slope * unclamped * on_top / (
        density * density * density
    )
    pair_square = pair_image.reshape(point_count, state_count, orbital_count, orbital_count)
    pair_sym = pair_square + jnp.swapaxes(pair_square, 2, 3)
    pair_grad = jnp.einsum("bspq,bq->bsp", pair_sym, orbitals, precision=highest)
    orbital_grad = grid_weights[:, None, None] * (
        pot_density[:, :, None] * density_grad + pot_pair[:, :, None] * pair_grad
    )
    return orbital_grad.reshape(point_count, state_count * orbital_count).astype(jnp.bfloat16)


def blocked_terms(orbitals, core_density, grid_weights, density_matrix, pair_matrix):
    point_count = orbitals.shape[0]
    row_block = 512
    block_count = point_count // row_block
    pieces = (
        orbitals.reshape(block_count, row_block, orbitals.shape[1]),
        core_density.reshape(block_count, row_block),
        grid_weights.reshape(block_count, row_block),
    )
    stacked = lax.map(
        lambda items: point_terms(items[0], items[1], items[2], density_matrix, pair_matrix), pieces
    )
    return stacked.reshape(point_count, stacked.shape[2])


def contract_rows(gradient, values):
    return lax.dot_general(
        gradient, values, (((0,), (0,)), ((), ())), preferred_element_type=jnp.float32
    )


def local(ao_values, coeffs, screen, core_density, grid_weights, density_matrix, pair_matrix):
    masked = mask_values(ao_values, screen)
    orbitals = lax.psum(jnp.dot(masked, coeffs, preferred_element_type=jnp.float32), "ao")
    gradient = blocked_terms(orbitals, core_density, grid_weights, density_matrix, pair_matrix)
    partial_pot = contract_rows(gradient, masked)
    return lax.psum(partial_pot, "grid")


bf16, f32 = jnp.bfloat16, jnp.float32
MESH = pl.DeviceIdType.MESH
AO, GRID = 4, 8
BLK = 128
CUT, DIRECT = 4, 0


def parts3(v):
    a = v.astype(bf16)
    r = v - a.astype(f32)
    b = r.astype(bf16)
    return a, b, (r - b.astype(f32)).astype(bf16)


def pair_row(index, act):
    first = index % act
    second = (first + index // act) % act
    return first * act + second, second * act + first


def ones_where(cond):
    return jnp.where(cond, 1.0, 0.0)


def kernel(ao_hbm, cf_hbm, screen_hbm, core_hbm, weights_hbm, dens_hbm, pair_hbm, out,
           ao, coeffs, screen, core_den, weights, dens, pair, mask, mcf, mat, pv, pvf, orot, dmat, dg,
           tgrad, top, den, grad, whole, s1_send, s1_recv, s2_send, s2_recv, s3_send, s3_recv,
           keep, gath, ld_sem, z_ss, z_rs, x_ss, x_rs):
    points, cols = ao.shape
    act = whole.shape[2]
    shifts = act // 2 + 1
    packed = shifts * act
    rows = dens.shape[0]
    states = rows // act
    pairs = act * act
    wide = AO * BLK
    groups = points // wide
    half, quarter, eighth = cols // 2, cols // 4, cols // 8
    za = lax.axis_index("ao")
    g = lax.axis_index("grid")
    core, x, y = lax.rem(g, 2), lax.rem(g // 2, 2), g // 4
    h = lax.rem(core + x + y, 2)
    b2 = x * (1 - h) + y * h
    b3 = y * (1 - h) + x * h
    p1 = g + 1 - 2 * core
    p2 = p1 + (1 - h) * (2 - 4 * x) + h * (4 - 8 * y)
    p3 = p1 + h * (2 - 4 * x) + (1 - h) * (4 - 8 * y)

    barrier = pltpu.get_barrier_semaphore()
    for k in range(1, AO):
        pl.semaphore_signal(barrier, inc=1, device_id={"ao": lax.rem(za + k, AO)}, device_id_type=MESH)
    p23 = g + 2 - 4 * x + 4 - 8 * y
    for p in (p1, p2, p3, p23):
        pl.semaphore_signal(barrier, inc=1, device_id={"grid": p}, device_id_type=MESH)

    def load(src, dst, i):
        cp = pltpu.make_async_copy(src, dst, ld_sem.at[i])
        cp.start()
        return cp

    step = 2 * BLK
    small = [load(s, d, i) for i, (s, d) in enumerate(((cf_hbm, coeffs), (screen_hbm, screen)))]
    count = points // step

    def ao_load(i):
        at = pl.ds(pl.multiple_of(i * step, step), step)
        return pltpu.make_async_copy(ao_hbm.at[at], ao.at[at], ld_sem.at[2 + i])

    for i in range(count):
        ao_load(i).start()
    late = [load(s, d, 2 + count + i) for i, (s, d) in enumerate(
        ((pair_hbm, pair), (dens_hbm, dens), (core_hbm, core_den), (weights_hbm, weights)))]

    for cp in small:
        cp.wait()
    cf = coeffs[...]
    marks = screen[...].astype(f32)
    for j in range(cols // BLK):
        v = jnp.broadcast_to(marks[:, j:j + 1], (points // BLK, BLK))
        for i in range(points // BLK):
            mask[i, :, j * BLK:(j + 1) * BLK] = jnp.broadcast_to(v[i:i + 1, :], (act, BLK)).astype(bf16)
    for i in range(points // BLK):
        mcf[i * act:(i + 1) * act, :] = cf * mask[i]

    def z_copy(src, dst, ss, rs, t, k):
        return pltpu.make_async_remote_copy(
            src_ref=src, dst_ref=dst, send_sem=ss.at[t, k - 1], recv_sem=rs.at[t, k - 1],
            device_id={"ao": lax.rem(za + k, AO)}, device_id_type=MESH)

    def whole_copy(t, k):
        return z_copy(whole.at[t, za], whole.at[t, za], z_ss, z_rs, t, k)

    def partial(t, c):
        for u in range(2):
            i = 2 * t + u
            ao_load(i).wait()
            r = lax.dot_general(mcf[pl.ds(pl.multiple_of(2 * i * act, 2 * act), 2 * act), :],
                                ao[pl.ds(pl.multiple_of(i * step, step), step), :],
                                (((1,), (1,)), ((), ())), preferred_element_type=f32)
            whole[t, za, :, u * step:u * step + BLK] = r[0:act, 0:BLK]
            whole[t, za, :, u * step + BLK:(u + 1) * step] = r[act:, BLK:]

        @pl.when(t == 0)
        def _():
            pl.semaphore_wait(barrier, AO - 1 + 4)

        for k in (2, 1, 3):
            whole_copy(t, k).start()
        return c

    lax.fori_loop(0, groups, partial, 0)
    for cp in late:
        cp.wait()
    d1, d2, d3 = parts3(dens[...])
    dmat[...] = jnp.concatenate([v.astype(f32) for v in (d1, d1, d2, d2, d1, d3)], axis=1).astype(bf16)
    fp, fq = pair_row(lax.broadcasted_iota(jnp.int32, (packed, pairs), 0), act)
    ci = lax.broadcasted_iota(jnp.int32, (packed, pairs), 1)
    fold_rows = (ones_where(ci == fp) + ones_where(ci == fq)).astype(bf16)
    few = 3
    for b in range(states // few):
        folded = jnp.dot(fold_rows, pair[:, b * few * pairs:(b + 1) * few * pairs], preferred_element_type=f32)
        hi = folded.astype(bf16)
        lo = (folded - hi.astype(f32)).astype(bf16)
        for i in range(few):
            mat[b * few + i, :, 0:pairs] = hi[:, i * pairs:(i + 1) * pairs]
            mat[b * few + i, :, pairs:] = lo[:, i * pairs:(i + 1) * pairs]

    def screen_rows(i, c):
        at = pl.multiple_of(i * BLK, BLK)
        for j in range(cols // BLK):
            m = jnp.concatenate([mask[i, :, j * BLK:(j + 1) * BLK]] * (BLK // mask.shape[1]), axis=0)
            ao[pl.ds(at, BLK), j * BLK:(j + 1) * BLK] = ao[pl.ds(at, BLK), j * BLK:(j + 1) * BLK] * m
        return c

    lax.fori_loop(0, points // BLK, screen_rows, 0)

    def prepare(t):
        o = orot[t, 0:act, :]
        for d in range(shifts):
            od = o if d == 0 else jnp.concatenate([o[d:], o[:d]], axis=0)
            if d:
                orot[t, d * act:(d + 1) * act, :] = od
            v = (o * od).astype(bf16)
            edge = d == 0 or d == shifts - 1
            pvf[t, d * act:(d + 1) * act, :] = v.astype(f32) * (0.5 if edge else 1.0)
        for p in range(act):
            v = (o[p:p + 1, :] * o).astype(bf16)
            pv[t, p * act:(p + 1) * act, :] = v
            pv[t, pairs + p * act:pairs + (p + 1) * act, :] = v
        o1, o2, o3 = parts3(o)
        dg[t] = jnp.dot(dmat[...], jnp.concatenate([o1, o2, o1, o2, o3, o1], axis=0), preferred_element_type=f32)

    def terms(t):
        o = orot[t, 0:act, :]
        image = jnp.dot(mat[...].reshape(states * packed, mat.shape[2]), pv[t], preferred_element_type=f32)
        for s in range(states):
            z = [image[s * packed + d * act:s * packed + (d + 1) * act, :] for d in range(shifts)]
            ot = z[0] * pvf[t, 0:act, :]
            tg = z[0] * o
            for d in range(1, shifts):
                ot = ot + z[d] * pvf[t, d * act:(d + 1) * act, :]
                tg = tg + z[d] * orot[t, d * act:(d + 1) * act, :]
            back = z[shifts - 2] * o
            for d in range(shifts - 3, -1, -1):
                back = jnp.concatenate([back[act - 1:], back[:act - 1]], axis=0)
                if d:
                    back = back + z[d] * o
            at = s * act
            tgrad[at:at + act, :] = tg + back
            top[s:s + 1, :] = jnp.sum(ot, axis=0, keepdims=True)
            den[s:s + 1, :] = jnp.sum(o * dg[t, at:at + act, :], axis=0, keepdims=True)
        start = pl.multiple_of(t * wide, wide)
        third = 1.0 / 3.0
        on_top = top[...]
        density = core_den[pl.ds(start, wide)].reshape(1, wide) + den[...]
        ratio = 4.0 * on_top / (density * density)
        unclamped = jnp.where(ratio < 1.0, 1.0, 0.0)
        polarize = jnp.sqrt(jnp.minimum(jnp.maximum(1.0 - ratio, 0.0), 1.0))
        upper = jnp.exp(jnp.log(1.0 + polarize) * third)
        lower = jnp.exp(jnp.log(1.0 - polarize) * third)
        u2, l2 = upper * upper, lower * lower
        enhance = u2 * u2 + l2 * l2
        slope = 4.0 / 3.0 / (u2 + upper * lower + l2)
        hc = jnp.exp(jnp.log(0.5 * density) * third)
        h2 = hc * hc
        base = 4.0 * slater_coef * (h2 * h2) * slope * unclamped / (density * density)
        pot_den = -(2.0 / 3.0) * slater_coef * hc * enhance - 2.0 * base * on_top / density
        w = weights[pl.ds(start, wide)].reshape(1, wide)
        top[...] = base * w
        den[...] = pot_den * w
        for s in range(states):
            at = s * act
            grad[at:at + act, pl.ds(start, wide)] = (
                den[s:s + 1, :] * dg[t, at:at + act, :] + top[s:s + 1, :] * tgrad[at:at + act, :]
            ).astype(bf16)

    cut = rows // CUT
    cuts = [slice(k * cut, (k + 1) * cut) for k in range(CUT)]
    sent = []

    def send(src, dst, p):
        i = len(sent)
        rc = pltpu.make_async_remote_copy(
            src_ref=src, dst_ref=dst, send_sem=x_ss.at[i], recv_sem=x_rs.at[i], device_id={"grid": p}, device_id_type=MESH)
        rc.start()
        sent.append(rc)
        return rc

    def pot(off):
        return jnp.dot(grad[...], ao[:, pl.ds(pl.multiple_of(off, eighth), quarter)], preferred_element_type=f32)

    def part(b):
        return pl.ds(pl.multiple_of(b * eighth, eighth), eighth)

    def entry_of(f2, f3):
        return h * 4 + lax.rem(b2 + f2, 2) * 2 + lax.rem(b3 + f3, 2)

    def write(e, r):
        out[r, part(e)] = gath[e, r].astype(f32)

    def share(e, r, p):
        return send(gath.at[e, r], gath.at[e, r], p)

    for t in range(groups):
        for k in range(1, AO):
            whole_copy(t, k).wait_recv()
        w = whole.at[t]
        orot[t, 0:act, :] = (w[0] + w[1]) + (w[2] + w[3])
        prepare(t)
        terms(t)

    own, other = h * half, (1 - h) * half
    c1, c2 = [], []

    def give(i, b):
        s1_send[i] = pot(other + b * quarter)
        for f in (1 - b2, b2):
            c1.append(send(s1_send.at[i, :, part(f)], s1_recv.at[i, :, part(f)], p1))

    give(0, 1 - b3)
    keep[0] = pot(own + (1 - b2) * quarter)
    for i, b in ((0, 1 - b3), (1, b3)):
        c1[i].wait_recv()
        for r in cuts:
            s2_send[i, r] = (keep[0, r, part(b)] + s1_recv[0, r, part(b)]).astype(bf16)
            c2.append(send(s2_send.at[i, r], s2_recv.at[i, r], p2))
    give(1, b3)
    keep[1] = pot(own + b2 * quarter)
    for i in range(2):
        c1[2 + i].wait_recv()
    keep[1] += s1_recv[1]
    c3 = []
    for k, r in enumerate(cuts):
        c2[k].wait_recv()
        s3_send[r] = (keep[1, r, part(1 - b3)] + s2_recv[0, r].astype(f32)).astype(bf16)
        c3.append(send(s3_send.at[r], s3_recv.at[r], p3))
    g1, g2, g3 = {}, {}, {}
    for k, r in enumerate(cuts):
        c2[CUT + k].wait_recv()
        c3[k].wait_recv()
        e = entry_of(0, 0)
        gath[e, r] = (keep[1, r, part(b3)] + s2_recv[1, r].astype(f32) + s3_recv[r].astype(f32)).astype(bf16)
        g3[k] = share(e, r, p3)
        if k >= CUT - DIRECT:
            g2[1, k] = share(e, r, p23)
        g1[0, k] = share(e, r, p1)
    for k, r in enumerate(cuts):
        e = entry_of(0, 0)
        g2[0, k] = share(e, r, p2)
        write(e, r)
    for k, r in enumerate(cuts):
        g3[k].wait_recv()
        e = entry_of(0, 1)
        if k < CUT - DIRECT:
            g2[1, k] = share(e, r, p2)
        g1[1, k] = share(e, r, p1)
        write(e, r)
    for k, r in enumerate(cuts):
        g2[0, k].wait_recv()
        e = entry_of(1, 0)
        g1[2, k] = share(e, r, p1)
        write(e, r)
    for k, r in enumerate(cuts):
        g2[1, k].wait_recv()
        e = entry_of(1, 1)
        g1[3, k] = share(e, r, p1)
        write(e, r)
    for i, (f2, f3) in enumerate(((0, 0), (0, 1), (1, 0), (1, 1))):
        e = (1 - h) * 4 + lax.rem(b3 + f2, 2) * 2 + lax.rem(b2 + f3, 2)
        for k, r in enumerate(cuts):
            g1[i, k].wait_recv()
            write(e, r)
    for t in range(groups):
        for k in range(1, AO):
            whole_copy(t, k).wait_send()
    for rc in sent:
        rc.wait_send()


def local_kernel(ao_values, coeffs, screen, core_density, grid_weights, density_matrix, pair_matrix):
    points, cols = ao_values.shape
    states, act = density_matrix.shape[0], density_matrix.shape[1]
    rows, pairs = states * act, act * act
    quarter, eighth = cols // 4, cols // 8
    blocks, wide = points // BLK, AO * BLK
    groups = points // wide
    packed = (act // 2 + 1) * act
    dma, V = pltpu.SemaphoreType.DMA, pltpu.VMEM
    args = (ao_values, coeffs.T, screen, core_density, grid_weights, density_matrix.reshape(rows, act), pair_matrix)
    return pl.pallas_call(
        kernel,
        out_shape=jax.ShapeDtypeStruct((rows, cols), f32),
        in_specs=[pl.BlockSpec(memory_space=pltpu.HBM)] * len(args),
        out_specs=pl.BlockSpec(memory_space=pltpu.VMEM),
        scratch_shapes=[
            V((points, cols), bf16), V((act, cols), bf16), V(screen.shape, jnp.int32), V((points,), f32), V((points,), f32),
            V((rows, act), f32), V(pair_matrix.shape, bf16), V((blocks, act, cols), bf16), V((blocks * act, cols), bf16),
            V((states, packed, 2 * pairs), bf16), V((groups, 2 * pairs, wide), bf16),
            V((groups, packed, wide), f32), V((groups, packed, wide), f32), V((rows, 6 * act), bf16), V((groups, rows, wide), f32),
            V((rows, wide), f32), V((states, wide), f32), V((states, wide), f32), V((rows, points), bf16),
            V((groups, AO, act, wide), f32),
            V((2, rows, quarter), f32), V((2, rows, quarter), f32),
            V((2, rows, eighth), bf16), V((2, rows, eighth), bf16), V((rows, eighth), bf16), V((rows, eighth), bf16),
            V((2, rows, quarter), f32), V((8, rows, eighth), bf16),
            dma((6 + points // (2 * BLK),)), dma((groups, AO - 1)), dma((groups, AO - 1)), dma((64,)), dma((64,)),
        ],
        compiler_params=pltpu.CompilerParams(
            collective_id=0, has_side_effects=True, vmem_limit_bytes=46 * 2**20),
    )(*[pltpu.with_memory_space_constraint(v, pltpu.HBM) for v in args])


def solution(mesh):
    fits = mesh.shape["grid"] == GRID and mesh.shape["ao"] == AO
    in_specs = (P("grid", "ao"), P("ao", None), P("grid", "ao"), P("grid"), P("grid"), P(), P())
    out_specs = P(None, "ao")
    return jax.shard_map(local_kernel if fits else local, mesh=mesh, in_specs=in_specs, out_specs=out_specs, check_vma=False)
```
